256 devices in a mesh: slab: 32 (over x_hi, z, core), coil: 8 (over x_lo, y).
Axes of the slice: x: 4 (x_hi: 2, x_lo: 2; x = x_hi * 2 + x_lo), y: 4, z: 8, core: 2. Of those that a mesh axis runs over, the one named last changes fastest.
Arguments:
- current_image: bfloat16 [8, 5, 2, 2, 256, 384], P('coil', None, None, None, 'slab'), may hold values from -6 to 6
- coil_maps: bfloat16 [32, 2, 2, 256, 384], P(None, None, None, 'slab'), may hold values from -2.5 to 2.5
- measured: bfloat16 [8, 32, 5, 2, 2, 384, 256], P('coil', 'slab'), may hold values from -4 to 4
- sampling: int32 [8, 5, 384, 256], P('coil'), may hold values 0 or 1
- first_weight: bfloat16 [64, 10, 3, 3, 3], replicated, may hold values from -0.375 to 0.375
- first_bias: float32 [64], replicated, may hold values from -3 to 3
- second_weight: bfloat16 [10, 64, 3, 3, 3], replicated, may hold values from -0.15625 to 0.15625
- second_bias: float32 [10], replicated, may hold values from -3 to 3
Outputs:
- refined: bfloat16 [8, 5, 2, 2, 256, 384], P('coil', None, None, None, 'slab')
The draws below stay inside these ranges and needn't reach their ends.
All inputs are finite; a program needn't handle non-finite values. No bound on the sum of `sampling` on one device may be relied on, other than what follows from the above.
Results may differ from the reference program's by a relative error of at most 0.014.
Values may be sent and summed in bfloat16 or wider, within the bound.
A program may use at most 128 MiB of HBM per device.

```python
import math
import jax
import jax.numpy as jnp
from jax import lax

WX = 2
E = 5
C = 32
NY = 384
NZ = 256
FEAT = 64
P_SIZE = 8


def with_ends(result, stream_key, smallest, largest):
    spot = [jax.random.randint(jax.random.fold_in(stream_key, axis), (), 0, length) for axis, length in enumerate(result.shape)]
    longest = result.shape.index(max(result.shape))
    beside = spot[:longest] + [(spot[longest] + 1) % result.shape[longest]] + spot[longest + 1:]
    return result.at[tuple(spot)].set(smallest).at[tuple(beside)].set(largest)


def block_scale(rng, extent, shards, smallest, top_value):
    gain, own = 1.0, jax.random.fold_in(rng, 6)
    for position, blocks in shards:
        heights = jnp.exp(jax.random.uniform(jax.random.fold_in(own, position), (blocks,), jnp.float32, smallest / len(shards), top_value / len(shards)))
        gain = gain * jnp.repeat(heights, extent[position] // blocks).reshape([-1 if axis == position else 1 for axis in range(len(extent))])
    return gain


def centred(rng, dims, scale, limit, pieces=(), kind=jnp.bfloat16):
    factor_of = block_scale(rng, dims, pieces, -0.22, 0.18) if pieces else 1.0
    array = jax.random.normal(rng, dims, jnp.float32) * scale * factor_of
    return jnp.minimum(jnp.maximum(array, -limit), limit).astype(kind)


def setup_inputs(seed: int = 0) -> dict:
    key_of = jax.random.split(jax.random.key(seed), 9)
    current_image = centred(key_of[0], (P_SIZE, E, 2, WX, NZ, NY), 1.0, 6.0, ((0, 8), (4, 32)))
    coil_maps = centred(key_of[1], (C, 2, WX, NZ, NY), 0.18, 2.5, ((3, 32),))
    measured = centred(key_of[2], (P_SIZE, C, E, 2, WX, NY, NZ), 0.25, 4.0, ((0, 8), (1, 32)))
    sampling = with_ends((jax.random.randint(key_of[3], (P_SIZE, E, NY, NZ), 0, 4) < 1).astype(jnp.int32), jax.random.fold_in(key_of[3], 1), 0, 1)
    first_weight = centred(key_of[4], (FEAT, 2 * E, 3, 3, 3), (54 * E) ** -0.5, 0.375)
    first_bias = centred(key_of[5], (FEAT,), 0.5, 3.0, (), jnp.float32)
    second_weight = centred(key_of[6], (2 * E, FEAT, 3, 3, 3), (27 * FEAT) ** -0.5, 0.15625)
    second_bias = centred(key_of[7], (2 * E,), 0.5, 3.0, (), jnp.float32)
    return {"current_image": current_image, "coil_maps": coil_maps, "measured": measured, "sampling": sampling, "first_weight": first_weight, "first_bias": first_bias, "second_weight": second_weight, "second_bias": second_bias}


def dft_table(length, inverse):
    indices = jnp.arange(length, dtype=jnp.int32)
    wrapped = indices[:, None] * indices[None, :] % length
    angles = wrapped.astype(jnp.float32) * (2.0 * math.pi / length)
    factor = 1.0 / math.sqrt(length)
    cosine = jnp.cos(angles) * factor
    sine_part = jnp.sin(angles) * factor
    phase_sign = 1.0 if inverse else -1.0
    upper_rows = jnp.stack([cosine, phase_sign * sine_part], axis=1)
    lower_rows = jnp.stack([-phase_sign * sine_part, cosine], axis=1)
    return jnp.stack([upper_rows, lower_rows], axis=0).astype(jnp.bfloat16)

def rounded(values):
    return lax.optimization_barrier(values.astype(jnp.bfloat16)).astype(jnp.float32)

def convolve_full(operand, weights):
    widened = jnp.pad(operand.astype(jnp.float32), ((0, 0), (0, 0), (0, 0), (0, 0), (1, 1)))
    return lax.conv_general_dilated(widened, weights.astype(jnp.float32), (1, 1, 1), 'VALID', dimension_numbers=('DCNHW', 'OIDHW', 'DCNHW'), precision=lax.Precision.HIGHEST)

def reference(current_image, coil_maps, measured, sampling, first_weight, first_bias, second_weight, second_bias):
    highest = lax.Precision.HIGHEST
    forward_y = dft_table(NY, False).astype(jnp.float32)
    inverse_y = dft_table(NY, True).astype(jnp.float32)
    forward_z = dft_table(NZ, False).astype(jnp.float32)
    inverse_z = dft_table(NZ, True).astype(jnp.float32)

    def one_phase(operands):
        image_phase, measured_phase, mask_phase = operands
        sampled = mask_phase.astype(jnp.float32)[:, None, None]
        image_wide = image_phase.astype(jnp.float32)

        def one_coil(running, coil_operands):
            maps_coil, measured_coil = coil_operands
            maps_wide = maps_coil.astype(jnp.float32)
            real_part = maps_wide[0] * image_wide[:, 0] - maps_wide[1] * image_wide[:, 1]
            imaginary_part = maps_wide[0] * image_wide[:, 1] + maps_wide[1] * image_wide[:, 0]
            products = rounded(jnp.stack([real_part, imaginary_part], axis=1))
            row_spectra = rounded(jnp.einsum('erxzy,ryqk->eqxzk', products, forward_y, precision=highest))
            spectrum = jnp.einsum('erxzk,rzqj->eqxkj', row_spectra, forward_z, precision=highest)
            residual = rounded(sampled * (spectrum - measured_coil.astype(jnp.float32)))
            depth_back = rounded(jnp.einsum('erxkj,rjqz->eqxzk', residual, inverse_z, precision=highest))
            image_back = jnp.einsum('erxzk,rkqy->eqxzy', depth_back, inverse_y, precision=highest)
            real_sum = maps_wide[0] * image_back[:, 0] + maps_wide[1] * image_back[:, 1]
            imaginary_sum = maps_wide[0] * image_back[:, 1] - maps_wide[1] * image_back[:, 0]
            return (running + jnp.stack([real_sum, imaginary_sum], axis=1), None)
        initial = jnp.zeros(image_phase.shape, jnp.float32)
        gradient, unused = lax.scan(one_coil, initial, (coil_maps, measured_phase))
        return (image_wide - gradient).astype(jnp.bfloat16)
    updated = lax.map(one_phase, (current_image, measured, sampling))
    stacked = updated.reshape((updated.shape[0], 2 * updated.shape[1]) + updated.shape[3:])
    padded = jnp.pad(stacked, ((1, 1), (0, 0), (0, 0), (1, 1), (0, 0)))
    hidden = jax.nn.relu(convolve_full(padded, first_weight) + first_bias[None, :, None, None, None])
    hidden = lax.optimization_barrier(hidden.astype(jnp.bfloat16))
    padded_hidden = jnp.pad(hidden, ((1, 1), (0, 0), (0, 0), (1, 1), (0, 0)))
    second = convolve_full(padded_hidden, second_weight)
    refined = stacked.astype(jnp.float32) + second + second_bias[None, :, None, None, None]
    return refined.astype(jnp.bfloat16).reshape(updated.shape)
```

```python
import functools
import math

import jax
import jax.numpy as jnp
import numpy as np
from jax import lax
from jax.experimental import pallas as pl
from jax.experimental.pallas import tpu as pltpu
from jax.sharding import PartitionSpec as P

MESH = pl.DeviceIdType.MESH
BF = jnp.bfloat16
F32 = jnp.float32
NY, NZ, E, FEAT = 384, 256, 5, 64
SLABS, PHASES = 32, 8


def dft_parts(length):
    indices = np.arange(length, dtype=np.int64)
    wrapped = indices[:, None] * indices[None, :] % length
    angles = wrapped.astype(np.float32) * np.float32(2.0 * math.pi / length)
    factor = np.float32(1.0 / math.sqrt(length))
    return np.cos(angles) * factor, np.sin(angles) * factor


def tables():
    cy, sy = dft_parts(NY)
    cz, sz = dft_parts(NZ)
    wy = np.block([[cy, sy], [-sy, cy]]).astype(jnp.bfloat16)
    wz = np.block([[cz, -sz], [sz, cz]]).astype(jnp.bfloat16)
    return wy, wz


def place():
    s = lax.axis_index("slab")
    p = lax.axis_index("coil")
    return s, p, s // 16, (s // 2) % 8, s % 2


def slab_of(xh, z, c):
    return xh * 16 + z * 2 + c


def rcopy(src, dst, ssem, rsem, s, p):
    return pltpu.make_async_remote_copy(
        src_ref=src,
        dst_ref=dst,
        send_sem=ssem,
        recv_sem=rsem,
        device_id={"slab": s, "coil": p},
        device_id_type=MESH,
    )


def gather_kernel(img, maps, G, M, xs, xr, rs, rr, cs, cr, s1s, s1r, s2s, s2r, ls):
    s, p, xh, z, c = place()
    sib = slab_of(xh, z, 1 - c)
    xp = slab_of(1 - xh, z, c)
    ring = [slab_of(xh, (z + 1) % 8, c), slab_of(xh, (z + 7) % 8, c)]
    barrier = pltpu.get_barrier_semaphore()

    def greet(a, b):
        pl.semaphore_signal(
            barrier, inc=1, device_id={"slab": a, "coil": b}, device_id_type=MESH
        )

    for a in (sib, xp, ring[0], ring[1]):
        greet(a, p)
    for q in range(1, 8):
        greet(s, (p + q) % 8)
    for j in range(4):
        delta = 4 * p + j

        @pl.when(delta != 0)
        def _():
            greet((s + 32 - delta) % 32, p)

    pl.semaphore_wait(barrier, 15 - jnp.where(p == 0, 1, 0))

    def slot(col, dz):
        return slab_of((xh + col) % 2, (z + dz) % 8, c)

    def ring_copy(src, col, d, t, k):
        if t == 4:
            src, dst = src.at[:, d], G.at[:, k, d]
        else:
            dst = G.at[:, k]
        return rcopy(src, dst, rs.at[col, d, t - 1], rr.at[col, d, t - 1], ring[d], p)

    def core_copy(src, col, dz, k):
        return rcopy(src, G.at[:, k], cs.at[col, dz], cr.at[col, dz], sib, p)

    sends = []

    def go(copy):
        copy.start()
        sends.append(copy)

    go(rcopy(img, G.at[:, s], xs, xr, xp, p))
    for d in range(2):
        go(ring_copy(img, 0, d, 1, s))
    own = pltpu.make_async_copy(img, G.at[:, s], ls.at[0])
    own.start()
    for j in range(4):
        delta = 4 * p + j
        far = (s + delta) % 32

        @pl.when(delta != 0)
        def _():
            rcopy(maps.at[far], M.at[s], s1s.at[j], s1r.at[j], far, p).start()

        @pl.when(delta == 0)
        def _():
            pltpu.make_async_copy(maps.at[s], M.at[s], ls.at[1]).start()

    go(core_copy(img, 0, 0, s))
    rcopy(img, G.at[:, xp], xs, xr, xp, p).wait_recv()
    for d in range(2):
        go(ring_copy(G.at[:, xp], 1, d, 1, xp))
    go(core_copy(G.at[:, xp], 1, 0, xp))
    for j in range(4):
        delta = 4 * p + j
        near = (s + 32 - delta) % 32

        @pl.when(delta != 0)
        def _():
            rcopy(maps.at[s], M.at[near], s1s.at[j], s1r.at[j], near, p).wait_recv()

        @pl.when(delta == 0)
        def _():
            pltpu.make_async_copy(maps.at[s], M.at[s], ls.at[1]).wait()

        for q in range(1, 8):
            go(rcopy(M.at[near], M.at[near], s2s.at[j, q - 1], s2r.at[j, q - 1], s, (p + q) % 8))
    for t in range(1, 5):
        for col in range(2):
            for d in range(2):
                dz = (8 - t) if d == 0 else t
                k = slot(col, dz)
                here = G.at[:, k]
                ring_copy(here, col, d, t, k).wait_recv()
                if t < 4:
                    go(ring_copy(here, col, d, t + 1, k))
                    go(core_copy(here, col, dz, k))
            if t == 4:
                k = slot(col, 4)
                go(core_copy(G.at[:, k], col, 4, k))
    for q in range(1, 8):
        for j in range(4):
            near = (s + 64 - (4 * ((p + 8 - q) % 8) + j)) % 32
            rcopy(M.at[near], M.at[near], s2s.at[j, q - 1], s2r.at[j, q - 1], s, p).wait_recv()
    for col in range(2):
        for dz in range(8):
            k = slab_of((xh + col) % 2, (z + dz) % 8, 1 - c)
            core_copy(G.at[:, k], col, dz, k).wait_recv()
    own.wait()
    for copy in sends:
        copy.wait_send()
    for j in range(4):
        delta = 4 * p + j
        far = (s + delta) % 32

        @pl.when(delta != 0)
        def _():
            rcopy(maps.at[far], M.at[s], s1s.at[j], s1r.at[j], far, p).wait_send()


def gather(img, maps):
    any_spec = pl.BlockSpec(memory_space=pl.ANY)
    sem = pltpu.SemaphoreType.DMA
    return pl.pallas_call(
        gather_kernel,
        out_shape=(
            jax.ShapeDtypeStruct((E, SLABS, 2, 2, 8, NY), BF),
            jax.ShapeDtypeStruct((SLABS, 2, 2, 8, NY), BF),
        ),
        in_specs=[any_spec] * 2,
        out_specs=(any_spec, any_spec),
        scratch_shapes=[
            sem,
            sem,
            sem((2, 2, 4)),
            sem((2, 2, 4)),
            sem((2, 8)),
            sem((2, 8)),
            sem((4,)),
            sem((4,)),
            sem((4, 7)),
            sem((4, 7)),
            sem((2,)),
        ],
        compiler_params=pltpu.CompilerParams(collective_id=0, has_side_effects=True),
        name="gather",
    )(img, maps)


NT = (((1,), (1,)), ((), ()))
NN = (((1,), (0,)), ((), ()))


def mm(a, b, dims):
    return lax.dot_general(a, b, dims, preferred_element_type=F32)


def dft_kernel(g_ref, m_ref, meas_ref, samp_ref, wy_ref, wz_ref, out_ref):
    mask = samp_ref[0].astype(F32)
    for x in range(2):
        wide = lambda v: v.astype(F32).reshape(NZ, NY)
        mr, mi = wide(m_ref[:, 0, x]), wide(m_ref[:, 1, x])
        ir, ii = wide(g_ref[0, :, 0, x]), wide(g_ref[0, :, 1, x])
        pr = (mr * ir - mi * ii).astype(BF)
        pi = (mr * ii + mi * ir).astype(BF)
        r = mm(wy_ref[...], jnp.concatenate([pr, pi], axis=1), NT).astype(BF)
        rc = jnp.concatenate([r[:NY], r[NY:]], axis=1)
        sp = mm(rc, wz_ref[...], NN)
        dr = (mask * (sp[:, :NZ] - meas_ref[0, 0, x].astype(F32))).astype(BF)
        di = (mask * (sp[:, NZ:] - meas_ref[0, 1, x].astype(F32))).astype(BF)
        b = mm(wz_ref[...], jnp.concatenate([dr, di], axis=1), NT).astype(BF)
        bc = jnp.concatenate([b[:NZ], b[NZ:]], axis=1)
        im = mm(bc, wy_ref[...], NN)
        br, bi = im[:, :NY], im[:, NY:]
        out_ref[0, :, 0, x] = (mr * br + mi * bi).reshape(SLABS, 8, NY).astype(BF)
        out_ref[0, :, 1, x] = (mr * bi - mi * br).reshape(SLABS, 8, NY).astype(BF)


def dft(G, M, meas, samp, wy, wz):
    whole = lambda shape: pl.BlockSpec(shape, lambda e: (0,) * len(shape))
    per_e = lambda shape: pl.BlockSpec((1,) + shape, lambda e: (e,) + (0,) * len(shape))
    return pl.pallas_call(
        dft_kernel,
        grid=(E,),
        out_shape=jax.ShapeDtypeStruct((E, SLABS, 2, 2, 8, NY), BF),
        in_specs=[
            per_e((SLABS, 2, 2, 8, NY)),
            whole((SLABS, 2, 2, 8, NY)),
            per_e((2, 2, NY, NZ)),
            per_e((NY, NZ)),
            whole((2 * NY, 2 * NY)),
            whole((2 * NZ, 2 * NZ)),
        ],
        out_specs=per_e((SLABS, 2, 2, 8, NY)),
        compiler_params=pltpu.CompilerParams(vmem_limit_bytes=60 * 1024 * 1024),
        name="dft",
    )(G, M, meas, samp, wy, wz)


def reduce_kernel(
    gd, img, U, H, sibbuf, S, rbuf, sbuf, xsb, xrb, esc, esend, erecv,
    cs, cr, rs, rr, xs, xr, es, er, us, ur, hs, hr,
):
    s, p, xh, z, c = place()
    sib = slab_of(xh, z, 1 - c)
    xp = slab_of(1 - xh, z, c)
    ring = [slab_of(xh, (z + 1) % 8, c), slab_of(xh, (z + 7) % 8, c)]
    has_up, has_down = s > 0, s < SLABS - 1
    has_before, has_after = p > 0, p < PHASES - 1
    barrier = pltpu.get_barrier_semaphore()

    def greet(a, b):
        pl.semaphore_signal(
            barrier, inc=1, device_id={"slab": a, "coil": b}, device_id_type=MESH
        )

    for a in (sib, xp, ring[0], ring[1]):
        greet(a, p)
    pl.when(has_up)(lambda: greet(s - 1, p))
    pl.when(has_down)(lambda: greet(s + 1, p))
    pl.when(has_before)(lambda: greet(s, p - 1))
    pl.when(has_after)(lambda: greet(s, p + 1))
    one = lambda cond: jnp.where(cond, 1, 0)
    pl.semaphore_wait(
        barrier, 4 + one(has_up) + one(has_down) + one(has_before) + one(has_after)
    )

    def sib_copy(e):
        return rcopy(gd.at[e, :, :, 1 - c], sibbuf.at[e], cs.at[e], cr.at[e], sib, p)

    def ring_copy(h, e, col, d):
        src, dst = sbuf.at[h, col, d, e], rbuf.at[h, col, d, e]
        if h == 0:
            src, dst = src.at[d], dst.at[d]
        return rcopy(src, dst, rs.at[h, col, d, e], rr.at[h, col, d, e], ring[d], p)

    def x_copy(e):
        return rcopy(xsb.at[e], xrb.at[e], xs.at[e], xr.at[e], xp, p)

    @pl.loop(0, E)
    def _(e):
        sib_copy(e).start()

    @pl.loop(0, E)
    def _(e):
        sib_copy(e).wait_recv()

        @pl.loop(0, 8)
        def _(zz):
            S[e, :, zz] = gd[e, :, zz, c].astype(F32) + sibbuf[e, :, zz].astype(F32)

        for col in range(2):
            for d in range(2):
                sbuf[0, col, d, e, d] = S[e, (xh + col) % 2, (z + 4) % 8, d].astype(BF)
                ring_copy(0, e, col, d).start()

    for h in range(1, 4):

        @pl.loop(0, E)
        def _(e):
            for col in range(2):
                for d in range(2):
                    ring_copy(h - 1, e, col, d).wait_recv()
                    k = 4 - h
                    tz = (z + k) % 8 if d == 0 else (z + 8 - k) % 8
                    lane = (xh + col) % 2
                    if h == 1:
                        v = S[e, lane, tz, d] + rbuf[0, col, d, e, d].astype(F32)
                        sbuf[1, col, d, e, d] = v.astype(BF)
                        sbuf[1, col, d, e, 1 - d] = S[e, lane, tz, 1 - d].astype(BF)
                    else:
                        v = S[e, lane, tz] + rbuf[h - 1, col, d, e].astype(F32)
                        sbuf[h, col, d, e] = v.astype(BF)
                    ring_copy(h, e, col, d).start()

    @pl.loop(0, E)
    def _(e):
        for col in (1, 0):
            for d in range(2):
                ring_copy(3, e, col, d).wait_recv()
            lane = (xh + col) % 2
            v = S[e, lane, z] + rbuf[3, col, 0, e].astype(F32) + rbuf[3, col, 1, e].astype(F32)
            if col == 1:
                xsb[e] = v.astype(BF)
                x_copy(e).start()
            else:
                S[e, lane, z] = v

    @pl.loop(0, E)
    def _(e):
        x_copy(e).wait_recv()
        g = S[e, xh, z] + xrb[e].astype(F32)
        u = (img[e].astype(F32) - g).astype(BF)
        U[2, e] = u
        v = u.astype(F32)
        for x in range(2):
            esc[e, :, 4 * x : 4 * x + 2] = v[:, x, 6:8]
            esc[e, :, 4 * x + 2 : 4 * x + 4] = v[:, x, 0:2]
        esend[e] = esc[e].astype(BF)

    def u_copy(i):
        src, dst, q = ((2, 1, p + 1), (2, 3, p - 1), (1, 0, p + 1), (3, 4, p - 1))[i]
        return rcopy(U.at[src], U.at[dst], us.at[i], ur.at[i], s, q)

    def h_copy(i):
        src, dst, q = ((2, 1, p + 1), (2, 3, p - 1), (1, 0, p + 1), (3, 4, p - 1))[i]
        return rcopy(H.at[src], H.at[dst], hs.at[i], hr.at[i], s, q)

    def e_copy(i):
        return rcopy(esend, erecv.at[i], es.at[i], er.at[i], (s + 1, s - 1)[i], p)

    through_up = jnp.logical_and(has_before, has_after)
    pl.when(has_down)(lambda: e_copy(0).start())
    pl.when(has_up)(lambda: e_copy(1).start())
    pl.when(has_after)(lambda: u_copy(0).start())
    pl.when(has_before)(lambda: u_copy(1).start())
    pl.when(has_up)(lambda: e_copy(0).wait_recv())
    pl.when(has_down)(lambda: e_copy(1).wait_recv())
    row = lax.broadcasted_iota(jnp.int32, (2, 8, NY), 1) % 4
    for e in range(E):
        up = jnp.where(has_up, erecv[0, e].astype(F32), 0.0)
        down = jnp.where(has_down, erecv[1, e].astype(F32), 0.0)
        H[2, e] = jnp.where(row < 2, up, down).astype(BF)
    pl.when(has_after)(lambda: h_copy(0).start())
    pl.when(has_before)(lambda: h_copy(1).start())
    for copy in (u_copy, h_copy):
        pl.when(has_before)(lambda: copy(0).wait_recv())
        pl.when(through_up)(lambda: copy(2).start())
        pl.when(has_after)(lambda: copy(1).wait_recv())
        pl.when(through_up)(lambda: copy(3).start())
    for copy in (u_copy, h_copy):
        pl.when(p > 1)(lambda: copy(2).wait_recv())
        pl.when(p < PHASES - 2)(lambda: copy(3).wait_recv())

    @pl.loop(0, E)
    def _(e):
        sib_copy(e).wait_send()
        x_copy(e).wait_send()
        for h in range(4):
            for col in range(2):
                for d in range(2):
                    ring_copy(h, e, col, d).wait_send()

    pl.when(has_down)(lambda: e_copy(0).wait_send())
    pl.when(has_up)(lambda: e_copy(1).wait_send())
    for copy in (u_copy, h_copy):
        pl.when(has_after)(lambda: copy(0).wait_send())
        pl.when(has_before)(lambda: copy(1).wait_send())
        pl.when(through_up)(lambda: copy(2).wait_send())
        pl.when(through_up)(lambda: copy(3).wait_send())


def reduce(gd, img):
    sem = pltpu.SemaphoreType.DMA
    vm = pl.BlockSpec(memory_space=pltpu.VMEM)
    return pl.pallas_call(
        reduce_kernel,
        out_shape=(
            jax.ShapeDtypeStruct((5, E, 2, 2, 8, NY), BF),
            jax.ShapeDtypeStruct((5, E, 2, 8, NY), BF),
        ),
        in_specs=[vm, vm],
        out_specs=(vm, vm),
        scratch_shapes=[
            pltpu.VMEM((E, 2, 8, 2, 2, 8, NY), BF),
            pltpu.VMEM((E, 2, 8, 2, 2, 8, NY), F32),
            pltpu.VMEM((4, 2, 2, E, 2, 2, 8, NY), BF),
            pltpu.VMEM((4, 2, 2, E, 2, 2, 8, NY), BF),
            pltpu.VMEM((E, 2, 2, 8, NY), BF),
            pltpu.VMEM((E, 2, 2, 8, NY), BF),
            pltpu.VMEM((E, 2, 8, NY), F32),
            pltpu.VMEM((E, 2, 8, NY), BF),
            pltpu.VMEM((2, E, 2, 8, NY), BF),
            sem((E,)),
            sem((E,)),
            sem((4, 2, 2, E)),
            sem((4, 2, 2, E)),
            sem((E,)),
            sem((E,)),
            sem((2,)),
            sem((2,)),
            sem((4,)),
            sem((4,)),
            sem((4,)),
            sem((4,)),
        ],
        compiler_params=pltpu.CompilerParams(
            collective_id=1, has_side_effects=True, vmem_limit_bytes=60 * 1024 * 1024
        ),
        name="reduce",
    )(gd, img)


K1 = 9 * 10 * 16
K1P = 1536
K2 = 3 * 10 * FEAT


def conv_kernel(U, H, w1_ref, b1_ref, w2_ref, b2_ref, out_ref, W1, W2, col, V, hid, osc):
    s = lax.axis_index("slab")
    p = lax.axis_index("coil")
    base = w1_ref[...].astype(F32)
    for zo in range(10):
        turned = base if zo == 0 else pltpu.roll(base, zo, 1)
        W1[zo * FEAT : (zo + 1) * FEAT, :] = turned[:, :K1].astype(BF)
    for d in range(3):
        base2 = w2_ref[d].astype(F32)
        for zz in range(8):
            turned = base2 if zz == 0 else pltpu.roll(base2, zz * FEAT, 1)
            W2[d * 128 + zz * 16 : d * 128 + zz * 16 + 16, :] = turned.astype(BF)
    lane = lax.broadcasted_iota(jnp.int32, (160, NY), 1)
    col[...] = jnp.zeros_like(col)
    for q in range(5):
        there = jnp.logical_and(p + q >= 2, p + q < PHASES + 2)
        for x in range(2):
            halo = H[q].reshape(10, 8, NY).astype(F32)
            col[:, 2:10] = U[q, :, :, x].reshape(10, 8, NY).astype(F32)
            col[:, 0:2] = halo[:, 4 * x : 4 * x + 2]
            col[:, 10:12] = halo[:, 4 * x + 2 : 4 * x + 4]
            v = jnp.where(there, col[...].reshape(160, NY), 0.0)
            back = jnp.where(lane == 0, 0.0, pltpu.roll(v, 1, 1))
            ahead = jnp.where(lane == NY - 1, 0.0, pltpu.roll(v, NY - 1, 1))
            for d, part in enumerate((back, v, ahead)):
                first = (q * 3 + d) * 160
                V[first : first + 160, x * NY : (x + 1) * NY] = part.astype(BF)
    rows = lax.broadcasted_iota(jnp.int32, (640, 2 * NY), 0)
    lowest = jnp.where(s == 0, FEAT, 0)
    highest = jnp.where(s == SLABS - 1, 9 * FEAT, 10 * FEAT)
    for t in range(3):
        there = jnp.logical_and(p + t >= 1, p + t < PHASES + 1)
        h = mm(W1[...], V[t * 480 : t * 480 + K1, :], NN) + b1_ref[...]
        keep = jnp.logical_and(jnp.logical_and(rows >= lowest, rows < highest), there)
        hid[t * 640 : (t + 1) * 640, :] = jnp.where(keep, jnp.maximum(h, 0.0), 0.0).astype(BF)
    o = mm(W2[...], hid[...], NN)
    lane2 = lax.broadcasted_iota(jnp.int32, (128, 2 * NY), 1) % NY
    total = (
        o[128:256]
        + jnp.where(lane2 == 0, 0.0, pltpu.roll(o[:128], 1, 1))
        + jnp.where(lane2 == NY - 1, 0.0, pltpu.roll(o[256:], 2 * NY - 1, 1))
    )
    for k in range(6):
        osc[k] = total[:, k * 128 : (k + 1) * 128]
    for i in range(10):
        for x in range(2):
            second = jnp.concatenate(
                [osc[3 * x + k, pl.ds(i, 8, stride=16), :] for k in range(3)], axis=1
            )
            v = U[2, i // 2, i % 2, x].astype(F32) + second + b2_ref[i]
            out_ref[i // 2, i % 2, x] = v.astype(BF)


def conv(U, H, first_weight, first_bias, second_weight, second_bias):
    w1 = first_weight.transpose(0, 2, 4, 1, 3)
    w1 = jnp.pad(w1, ((0, 0),) * 4 + ((0, 13),)).reshape(FEAT, K1)
    w1 = jnp.pad(w1, ((0, 0), (0, K1P - K1)))
    w2 = second_weight.transpose(4, 0, 2, 3, 1)
    w2 = jnp.pad(w2, ((0, 0), (0, 6), (0, 0), (0, 7), (0, 0))).reshape(3, 16, K2)
    b1 = jnp.tile(first_bias, 10)[:, None]
    vm = pl.BlockSpec(memory_space=pltpu.VMEM)
    return pl.pallas_call(
        conv_kernel,
        out_shape=jax.ShapeDtypeStruct((E, 2, 2, 8, NY), BF),
        in_specs=[vm, vm, vm, vm, vm, pl.BlockSpec(memory_space=pltpu.SMEM)],
        out_specs=vm,
        scratch_shapes=[
            pltpu.VMEM((640, K1), BF),
            pltpu.VMEM((384, K2), BF),
            pltpu.VMEM((10, 16, NY), F32),
            pltpu.VMEM((2400, 2 * NY), BF),
            pltpu.VMEM((1920, 2 * NY), BF),
            pltpu.VMEM((6, 128, 128), F32),
        ],
        compiler_params=pltpu.CompilerParams(vmem_limit_bytes=60 * 1024 * 1024),
        name="conv",
    )(U, H, w1, b1, w2, second_bias)


def on_device(
    current_image,
    coil_maps,
    measured,
    sampling,
    first_weight,
    first_bias,
    second_weight,
    second_bias,
):
    wy, wz = tables()
    img = current_image[0]
    G, M = gather(img, coil_maps)
    gd = dft(G, M, measured[0, 0], sampling[0], jnp.asarray(wy), jnp.asarray(wz))
    U, H = reduce(gd.reshape(E, 2, 8, 2, 2, 2, 8, NY), img)
    out = conv(U, H, first_weight, first_bias, second_weight, second_bias)
    return out[None]


def solution(mesh):
    in_specs = (
        P("coil", None, None, None, "slab", None),
        P(None, None, None, "slab", None),
        P("coil", "slab", None, None, None, None, None),
        P("coil", None, None, None),
        P(),
        P(),
        P(),
        P(),
    )
    out_specs = P("coil", None, None, None, "slab", None)
    return jax.shard_map(
        on_device, mesh=mesh, in_specs=in_specs, out_specs=out_specs, check_vma=False
    )
```

```python
import functools
import math

import jax
import jax.numpy as jnp
import numpy as np
from jax import lax
from jax.experimental import pallas as pl
from jax.experimental.pallas import tpu as pltpu
from jax.sharding import PartitionSpec as P

MESH = pl.DeviceIdType.MESH
BF = jnp.bfloat16
F32 = jnp.float32
NY, NZ, E, FEAT = 384, 256, 5, 64
SLABS, PHASES = 32, 8
NT = (((1,), (1,)), ((), ()))
NN = (((1,), (0,)), ((), ()))
OFFSETS = (1, -1, 2, -2)
SHARE = (4, 1, 7, 3, 5, 2, 6)
KA, KB = 9 * 8 * 16, 9 * 2 * 16
K2 = 3 * 10 * FEAT


def dft_parts(length):
    indices = np.arange(length, dtype=np.int64)
    wrapped = indices[:, None] * indices[None, :] % length
    angles = wrapped.astype(np.float32) * np.float32(2.0 * math.pi / length)
    factor = np.float32(1.0 / math.sqrt(length))
    return np.cos(angles) * factor, np.sin(angles) * factor


def tables():
    cy, sy = dft_parts(NY)
    cz, sz = dft_parts(NZ)
    wy = np.stack([cy, sy]).astype(jnp.bfloat16)
    wz = np.stack([cz, sz]).astype(jnp.bfloat16)
    return wy, wz


def place():
    s = lax.axis_index("slab")
    p = lax.axis_index("coil")
    return s, p, s // 16, (s // 2) % 8, s % 2


def slab_of(xh, z, c):
    return xh * 16 + z * 2 + c


def rcopy(src, dst, ssem, rsem, s, p):
    return pltpu.make_async_remote_copy(
        src_ref=src,
        dst_ref=dst,
        send_sem=ssem,
        recv_sem=rsem,
        device_id={"slab": s, "coil": p},
        device_id_type=MESH,
    )


def mm(a, b, dims):
    return lax.dot_general(a, b, dims, preferred_element_type=F32)


STAGE = {1: ["m1"], 2: [("g", 0, 0, 1, 2)], 3: [("g", 0, 1, 1, 3)], 4: [("far", 0, 1)]}


class Plan:
    LINKS = {"z0": (0.5, 2.1), "z1": (0.5, 2.1), "x": (0.5, 3.0), "c": (0.05, 1.6),
             "y": (1.5, 3.2), "e": (0.5, 6.0), "m1": (0.5, 4.0), "m2": (0.3, 3.0)}

    def __init__(self):
        self.tasks = []

    def add(self, name, fn, after=(), needs=(), sends=(), cost=0.05, rank=0):
        self.tasks.append((name, fn, tuple(after), tuple(needs), tuple(sends), cost, rank))

    def run(self):
        now, done, arrive, free = 0.0, {}, {}, {}
        left = list(self.tasks)
        while left:
            best = None
            for i, (name, _, after, needs, _, _, rank) in enumerate(left):
                if any(a not in done for a in after) or any(m not in arrive for m in needs):
                    continue
                ready = max([0.0] + [arrive[m] for m in needs])
                key = (max(ready, now), rank, i)
                if best is None or key < best[0]:
                    best = (key, i)
            name, fn, _, _, sends, cost, _ = left.pop(best[1])
            now = best[0][0] + cost
            for message, link, size in sends:
                rate, lag = self.LINKS[link]
                free[link] = max(free.get(link, 0.0), now) + rate * size
                arrive[message] = free[link] + lag
            done[name] = now
            fn()
        return now


def kernel(
    img_h, maps, meas_h, samp_h, wy_h, wz_h, w1_ref, b1_ref, w2_ref, b2_ref, out_ref,
    img, G, M, meas, samp, wy, wz, gd, sibbuf, S, rbuf, sbuf, xsb, xrb, res, esc, esend, erecv, U,
    W1A, W1B, W2, b1_s, w2_s, col_s, VA, VB, hacc, hid, osc,
    xs, xr, rs, rr, cs, cr, s1s, s1r, s2s, s2r, ls,
    bcs, bcr, brs, brr, bxs, bxr, es, er, us, ur,
):
    s, p, xh, z, c = place()
    sib = slab_of(xh, z, 1 - c)
    xp = slab_of(1 - xh, z, c)
    ring = [slab_of(xh, (z + 1) % 8, c), slab_of(xh, (z + 7) % 8, c)]
    has_up, has_down = s > 0, s < SLABS - 1

    def phase_there(q):
        return jnp.logical_and(p + q >= 0, p + q < PHASES)

    loads = [
        pltpu.make_async_copy(a, b, ls.at[i])
        for i, (a, b) in enumerate(
            (
                (img_h, img),
                (wy_h.at[0], wy.at[0:NY, 0:NY]),
                (wy_h.at[0], wy.at[NY:, NY:]),
                (wy_h.at[1], wy.at[0:NY, NY:]),
                (wz_h.at[0], wz.at[0:NZ, 0:NZ]),
                (wz_h.at[0], wz.at[NZ:, NZ:]),
                (wz_h.at[1], wz.at[NZ:, 0:NZ]),
                (samp_h, samp),
                (meas_h, meas),
            )
        )
    ]
    for load in loads:
        load.start()

    def weights1():
        k = lax.broadcasted_iota(jnp.int32, (270, 1), 0)
        source = ((k // 9 % 3 * 3 + k % 3) * 10 + k // 27) * 16 + k // 3 % 3
        for W, n, wide, first in ((W1A, KA, 8, 0), (W1B, KB, 2, 8)):
            padded = -(-n // 128) * 128
            m = lax.broadcasted_iota(jnp.int32, (1, padded), 1)
            target = (m // (16 * wide) * 10 + first + m // 16 % wide) * 16 + m % 16
            pick = jnp.where(source == target, 1.0, 0.0).astype(BF)
            base = mm(w1_ref[...], pick, NN)
            for zo in range(10):
                turned = base if zo == 0 else pltpu.roll(base, zo, 1)
                W[zo * FEAT : (zo + 1) * FEAT, :] = turned[:, :n].astype(BF)
        same = lax.broadcasted_iota(jnp.int32, (FEAT, FEAT), 0) == lax.broadcasted_iota(
            jnp.int32, (FEAT, FEAT), 1
        )
        bias = jnp.sum(jnp.where(same, b1_ref[...], 0.0), axis=1, keepdims=True)
        for zo in range(10):
            b1_s[zo * FEAT : (zo + 1) * FEAT, :] = bias
        col_s[...] = jnp.zeros_like(col_s)

    def weights2(d):
        k = lax.broadcasted_iota(jnp.int32, (27 * FEAT, 1), 0)
        source = jnp.where(k % 3 == d, k // 3 % 9 * FEAT + k // 27, -1)
        m = lax.broadcasted_iota(jnp.int32, (1, 640), 1)
        pick = jnp.where(source == m, 1.0, 0.0).astype(BF)
        base = mm(w2_ref[...], pick, NN)
        w2_s[...] = jnp.zeros_like(w2_s)
        for a in range(3):
            w2_s[0:10, a * 640 : a * 640 + 192] = base[:, a * 192 : a * 192 + 192]
        base = w2_s[...]
        for zz in range(8):
            turned = base if zz == 0 else pltpu.roll(base, zz * FEAT, 1)
            W2[d * 128 + zz * 16 : d * 128 + zz * 16 + 16, :] = turned.astype(BF)

    barrier = pltpu.get_barrier_semaphore()

    def greet(a, b):
        pl.semaphore_signal(
            barrier, inc=1, device_id={"slab": a, "coil": b}, device_id_type=MESH
        )

    for a in (sib, xp, ring[0], ring[1]):
        greet(a, p)
    for q in range(1, 8):
        greet(s, (p + q) % 8)
    for q in (-2, -1, 0, 1, 2):
        pl.when(jnp.logical_and(has_up, phase_there(q)))(lambda: greet(s - 1, p + q))
        pl.when(jnp.logical_and(has_down, phase_there(q)))(lambda: greet(s + 1, p + q))
    for j in range(4):
        delta = p + 8 * j

        @pl.when(delta != 0)
        def _():
            greet((s + 32 - delta) % 32, p)

    one = lambda cond: jnp.where(cond, 1, 0)
    aside = sum(one(phase_there(q)) for q in OFFSETS)
    pl.semaphore_wait(
        barrier, 15 - one(p == 0) + one(has_up) * (aside + 1) + one(has_down) * (aside + 1)
    )

    plan = Plan()

    def near(j):
        return (s + 32 - (p + 8 * j)) % 32

    def maps_first():
        for j in range(4):
            delta = p + 8 * j
            far = (s + delta) % 32

            @pl.when(delta != 0)
            def _():
                rcopy(maps.at[far], M.at[s], s1s.at[j], s1r.at[j], far, p).start()

            @pl.when(delta == 0)
            def _():
                pltpu.make_async_copy(maps.at[s], M.at[s], ls.at[9]).start()

    def maps_share(j):
        delta = p + 8 * j
        k = near(j)

        @pl.when(delta != 0)
        def _():
            rcopy(maps.at[s], M.at[k], s1s.at[j], s1r.at[j], k, p).wait_recv()

        @pl.when(delta == 0)
        def _():
            pltpu.make_async_copy(maps.at[s], M.at[s], ls.at[9]).wait()

        for q in SHARE:
            maps_copy(j, q, k, 0).start()

    def maps_copy(j, q, k, x):
        half = M.at[k, :, x]
        return rcopy(half, half, s2s.at[x], s2r.at[x, j, q - 1], s, (p + q) % 8)

    def maps_rest():
        for j in range(4):
            for q in SHARE:
                maps_copy(j, q, near(j), 1).start()

    def maps_wait(x):
        for q in SHARE:
            for j in range(4):
                k = (s + 32 - ((p + 8 - q) % 8 + 8 * j)) % 32
                maps_copy(j, q, k, x).wait_recv()

    plan.add("m1", maps_first, after=[("own", 0)],
             sends=[("m1a", "z0", 4), ("m1b", "z1", 4), ("m1", "m1", 4)], rank=-3)
    for j in range(4):
        plan.add(("m2", j), lambda j=j: maps_share(j), after=["m1"], needs=["m1", "m1a", "m1b"],
                 sends=[(("m2", j), "m2", 3.5)], rank=-1)
    plan.add("m2b", maps_rest, after=[("m2", j) for j in range(4)], sends=[("m2b", "m2", 14)], rank=-1)

    def slot(col, dz):
        return slab_of((xh + col) % 2, (z + dz) % 8, c)

    def ring_copy(src, e, col, d, t, k):
        if t == 4:
            src, dst = src.at[d], G.at[e, k, d]
        else:
            dst = G.at[e, k]
        return rcopy(src, dst, rs.at[e], rr.at[e, col, d, t - 1], ring[d], p)

    def core_copy(src, e, k):
        return rcopy(src, G.at[e, k], cs.at[e], cr.at[e], sib, p)

    def own_start(e):
        for d in range(2):
            ring_copy(img_h.at[e], e, 0, d, 1, s).start()

    def own_aside():
        for e in range(E):
            rcopy(img_h.at[e], G.at[e, s], xs.at[e], xr.at[e], xp, p).start()
        for e in range(E):
            core_copy(img_h.at[e], e, s).start()
            G[e, s] = img[e]

    def cross(e):
        rcopy(img_h.at[e], G.at[e, xp], xs.at[e], xr.at[e], xp, p).wait_recv()
        for d in range(2):
            ring_copy(G.at[e, xp], e, 1, d, 1, xp).start()
        core_copy(G.at[e, xp], e, xp).start()

    def hop(e, col, d, t):
        k = slot(col, (8 - t) if d == 0 else t)
        here = G.at[e, k]
        ring_copy(here, e, col, d, t, k).wait_recv()
        if t < 4:
            ring_copy(here, e, col, d, t + 1, k).start()
            core_copy(here, e, k).start()

    def far_slab(e, col):
        for d in range(2):
            hop(e, col, d, 4)
        k = slot(col, 4)
        core_copy(G.at[e, k], e, k).start()

    def gathered(e):
        rcopy(G.at[e, 0:16], G.at[e, 0:16], cs.at[e], cr.at[e], sib, p).wait_recv()

    plan.add("img", lambda: loads[0].wait(), cost=0.3, rank=-2)
    plan.add("aside", own_aside, after=["m1", "img"], sends=[(("x", e), "x", 1) for e in range(E)], rank=-2)
    for e in range(E):
        plan.add(("own", e), lambda e=e: own_start(e), after=["img"] + STAGE.get(e, []),
                 sends=[(("g", e, 0, 0, 1), "z0", 1), (("g", e, 0, 1, 1), "z1", 1)],
                 rank=-2 if e < 1 else e)
        plan.add(("cross", e), lambda e=e: cross(e), after=[("own", e)], needs=[("x", e)],
                 sends=[(("g", e, 1, 0, 1), "z0", 1), (("g", e, 1, 1, 1), "z1", 1)], rank=e)
        for col in range(2):
            for t in range(1, 4):
                for d in range(2):
                    m = ("g", e, col, d, t)
                    plan.add(m, lambda e=e, col=col, d=d, t=t: hop(e, col, d, t), needs=[m],
                             sends=[(("g", e, col, d, t + 1), "z%d" % d, 0.5 if t == 3 else 1)], rank=e)
            plan.add(("far", e, col), lambda e=e, col=col: far_slab(e, col),
                     after=[("g", e, k, d, t) for k in range(col + 1) for d in range(2) for t in range(1, 4)],
                     needs=[("g", e, col, 0, 4), ("g", e, col, 1, 4)],
                     sends=[(("far", e, col), "c", 1)], rank=e)
        plan.add(("full", e), lambda e=e: gathered(e), after=[("far", e, 0), ("far", e, 1)],
                 needs=[("far", e, 0), ("far", e, 1)], rank=e)

    def tables_wait():
        for load in loads[1:]:
            load.wait()
        wy[NY:, 0:NY] = -wy[0:NY, NY:]
        wz[0:NZ, NZ:] = -wz[NZ:, 0:NZ]
        maps_wait(0)

    plan.add("tables", tables_wait, after=[("m2", j) for j in range(4)],
             needs=[("m2", j) for j in range(4)], rank=0)

    plan.add("maps1", lambda: maps_wait(1), needs=["m2b"], after=["tables"], rank=0)
    plan.add("w1", weights1, after=[("own", 1)], cost=2.0, rank=6)
    for d in range(3):
        plan.add(("w2", d), lambda d=d: weights2(d), after=["w1"], cost=1.8, rank=7)

    def block(e, x):
        mask = samp[e].astype(F32)
        wide = lambda v: v.astype(F32).reshape(NZ, NY)
        mr, mi = wide(M[:, 0, x]), wide(M[:, 1, x])
        ir, ii = wide(G[e, :, 0, x]), wide(G[e, :, 1, x])
        pr = (mr * ir - mi * ii).astype(BF)
        pi = (mr * ii + mi * ir).astype(BF)
        r = mm(wy[...], jnp.concatenate([pr, pi], axis=1), NT).astype(BF)
        rc = jnp.concatenate([r[:NY], r[NY:]], axis=1)
        sp = mm(rc, wz[...], NN)
        dr = (mask * (sp[:, :NZ] - meas[e, 0, x].astype(F32))).astype(BF)
        di = (mask * (sp[:, NZ:] - meas[e, 1, x].astype(F32))).astype(BF)
        res[:, :NZ] = dr
        res[:, NZ:] = di

    def block_back(e, x):
        wide = lambda v: v.astype(F32).reshape(NZ, NY)
        mr, mi = wide(M[:, 0, x]), wide(M[:, 1, x])
        b = mm(wz[...], res[...], NT).astype(BF)
        bc = jnp.concatenate([b[:NZ], b[NZ:]], axis=1)
        im = mm(bc, wy[...], NN)
        br, bi = im[:, :NY], im[:, NY:]
        cells = (2, 8, 2, 8, NY)
        gd[e, :, :, :, 0, x] = (mr * br + mi * bi).reshape(cells).astype(BF)
        gd[e, :, :, :, 1, x] = (mr * bi - mi * br).reshape(cells).astype(BF)

    def sib_copy(e):
        return rcopy(gd.at[e, :, :, 1 - c], sibbuf.at[e], bcs.at[e], bcr.at[e], sib, p)

    def last_block(e):
        block_back(e, 1)
        sib_copy(e).start()

    def back_copy(h, e, col, d):
        src, dst = sbuf.at[h, col, d, e], rbuf.at[h, col, d, e]
        if h == 0:
            src, dst = src.at[d], dst.at[d]
        return rcopy(src, dst, brs.at[e], brr.at[h, col, d, e], ring[d], p)

    def x_copy(e):
        return rcopy(xsb.at[e], xrb.at[e], bxs.at[e], bxr.at[e], xp, p)

    def pair_sum(e):
        sib_copy(e).wait_recv()
        S[e] = gd[e, :, :, c].astype(F32) + sibbuf[e].astype(F32)
        for col in (1, 0):
            for d in range(2):
                sbuf[0, col, d, e, d] = S[e, (xh + col) % 2, (z + 4) % 8, d].astype(BF)
                back_copy(0, e, col, d).start()

    def back_hop(e, h, col):
        for d in range(2):
            back_copy(h - 1, e, col, d).wait_recv()
            k = 4 - h
            tz = (z + k) % 8 if d == 0 else (z + 8 - k) % 8
            lane = (xh + col) % 2
            if h == 1:
                v = S[e, lane, tz, d] + rbuf[0, col, d, e, d].astype(F32)
                sbuf[1, col, d, e, d] = v.astype(BF)
                sbuf[1, col, d, e, 1 - d] = S[e, lane, tz, 1 - d].astype(BF)
            else:
                v = S[e, lane, tz] + rbuf[h - 1, col, d, e].astype(F32)
                sbuf[h, col, d, e] = v.astype(BF)
            back_copy(h, e, col, d).start()

    def back_end(e, col):
        for d in range(2):
            back_copy(3, e, col, d).wait_recv()
        lane = (xh + col) % 2
        v = S[e, lane, z] + rbuf[3, col, 0, e].astype(F32) + rbuf[3, col, 1, e].astype(F32)
        if col == 1:
            xsb[e] = v.astype(BF)
            x_copy(e).start()
        else:
            S[e, lane, z] = v

    def u_copy(i, e):
        q = OFFSETS[i]
        return rcopy(U.at[2, e], U.at[2 - q, e], us.at[i, e], ur.at[i, e], s, p + q)

    def e_copy(i, q, e):
        k = 5 * i + q + 2
        return rcopy(esend.at[i, e], erecv.at[i, 2 - q, e], es.at[k, e], er.at[k, e], (s + 1, s - 1)[i], p + q)

    def all_halo(act, inward):
        for i, q in enumerate(OFFSETS):
            pl.when(phase_there(-q if inward else q))(lambda: act(lambda e: u_copy(i, e)))
        for i, cond in enumerate((has_up, has_down) if inward else (has_down, has_up)):
            for q in (0, -1, 1, -2, 2):
                both = jnp.logical_and(cond, phase_there(-q if inward else q))
                pl.when(both)(lambda: act(lambda e: e_copy(i, q, e)))

    def update(e):
        x_copy(e).wait_recv()
        g = S[e, xh, z] + xrb[e].astype(F32)
        u = (img[e].astype(F32) - g).astype(BF)
        U[2, e] = u
        v = u.astype(F32)
        for i, first in enumerate((6, 0)):
            for r in range(2):
                for x in range(2):
                    k = 4 * r + 2 * x
                    esc[i, e, k : k + 2] = v[r, x, first : first + 2]
            esend[i, e] = esc[i, e].astype(BF)
        all_halo(lambda copy: copy(e).start(), False)

    lane = lax.broadcasted_iota(jnp.int32, (32, NY), 1)

    def columns(e):
        all_halo(lambda copy: copy(e).wait_recv(), True)
        V, rows, part0 = (VB, 32, 0) if isinstance(e, int) else (VA, 128, e * 32)

        @pl.loop(0, 5)
        def _(q):
            there = jnp.logical_and(p + q >= 2, p + q < PHASES + 2)
            up = jnp.where(has_up, erecv[0, q, e].astype(F32), 0.0)
            down = jnp.where(has_down, erecv[1, q, e].astype(F32), 0.0)
            for x in range(2):
                col_s[:, 2:10] = U[q, e, :, x].astype(F32)
                for r in range(2):
                    k = 4 * r + 2 * x
                    col_s[r, 0:2] = up[k : k + 2]
                    col_s[r, 10:12] = down[k : k + 2]
                v = jnp.where(there, col_s[...].reshape(32, NY), 0.0)
                back = jnp.where(lane == 0, 0.0, pltpu.roll(v, 1, 1))
                ahead = jnp.where(lane == NY - 1, 0.0, pltpu.roll(v, NY - 1, 1))
                for d, part in enumerate((back, v, ahead)):
                    first = pl.multiple_of((q * 3 + d) * rows + part0, 32)
                    V[pl.ds(first, 32), x * NY : (x + 1) * NY] = part.astype(BF)

    def conv_part(t):
        hacc[t] = mm(W1A[...], VA[t * 384 : t * 384 + KA, :], NN) + b1_s[...]

    before = []
    later = ["maps1"]
    for e in range(E):
        for x in range(2):
            plan.add(("dft", e, x), lambda e=e, x=x: block(e, x), after=["tables", ("full", e)] + before + later * x,
                     cost=0.93, rank=20 + e)
            before = [("back", e, x)]
            plan.add(before[0], lambda e=e, x=x: last_block(e) if x else block_back(e, 0),
                     after=[("dft", e, x)], cost=0.93, sends=[(("bc", e), "c", 16)] * x, rank=20 + e)
        plan.add(("pair", e), lambda e=e: pair_sum(e), after=[("back", e, 1)], needs=[("bc", e)], cost=0.25,
                 sends=[(("b", e, col, 0), "z%d" % d, 0.5) for col in (1, 0) for d in range(2)], rank=10 + e)
        for h in range(1, 4):
            for col in (1, 0):
                plan.add(("back", e, h, col), lambda e=e, h=h, col=col: back_hop(e, h, col),
                         needs=[("b", e, col, h - 1)], after=[("pair", e)] + [("back", e, h, 1)] * (1 - col),
                         sends=[(("b", e, col, h), "z%d" % d, 1) for d in range(2)], cost=0.03, rank=10 + e)
        for col in (1, 0):
            plan.add(("end", e, col), lambda e=e, col=col: back_end(e, col), needs=[("b", e, col, 3)],
                     after=[("back", e, 3, col)], sends=[(("bx", e), "x", 1)] * col, cost=0.1, rank=10 + e)
        plan.add(("upd", e), lambda e=e: update(e), needs=[("bx", e)], after=[("end", e, 0)], cost=0.05,
                 sends=[(("e", e), "e", 1), (("u", e), "y", 1)], rank=10 + e)
    plan.add("cols", lambda: pl.loop(0, 4)(columns), needs=[(k, 3) for k in "ue"], after=[("upd", 4)], cost=1.0)
    for t in range(3):
        plan.add(("conv", t), lambda t=t: conv_part(t), after=["cols"], cost=1.9, rank=30)
    plan.add("cols4", lambda: columns(4), needs=[(k, 4) for k in "ue"], after=["cols"], cost=0.25, rank=40)

    plan.run()

    rows = lax.broadcasted_iota(jnp.int32, (640, 2 * NY), 0)
    lowest = jnp.where(s == 0, FEAT, 0)
    highest = jnp.where(s == SLABS - 1, 9 * FEAT, 10 * FEAT)
    for t in range(3):
        there = jnp.logical_and(p + t >= 1, p + t < PHASES + 1)
        h = mm(W1B[...], VB[t * 96 : t * 96 + KB, :], NN) + hacc[t]
        keep = jnp.logical_and(jnp.logical_and(rows >= lowest, rows < highest), there)
        hid[t * 640 : (t + 1) * 640, :] = jnp.where(keep, jnp.maximum(h, 0.0), 0.0).astype(BF)
    o = mm(W2[...], hid[...], NN)
    lane2 = lax.broadcasted_iota(jnp.int32, (128, 2 * NY), 1) % NY
    total = (
        o[128:256]
        + jnp.where(lane2 == 0, 0.0, pltpu.roll(o[:128], 1, 1))
        + jnp.where(lane2 == NY - 1, 0.0, pltpu.roll(o[256:], 2 * NY - 1, 1))
    )
    for k in range(6):
        osc[k] = total[:, k * 128 : (k + 1) * 128]
    for i in range(10):
        for x in range(2):
            second = jnp.concatenate(
                [osc[3 * x + k, pl.ds(i, 8, stride=16), :] for k in range(3)], axis=1
            )
            v = U[2, i // 2, i % 2, x].astype(F32) + second + b2_ref[i]
            out_ref[i // 2, i % 2, x] = v.astype(BF)

    for j in range(4):
        delta = p + 8 * j
        far = (s + delta) % 32

        @pl.when(delta != 0)
        def _():
            rcopy(maps.at[far], M.at[s], s1s.at[j], s1r.at[j], far, p).wait_send()

    for x in range(2):
        rcopy(G.at[0, 0:14], G.at[0, 0:14], s2s.at[x], s2r.at[0, 0, 0], s, p).wait_send()

    @pl.loop(0, E)
    def _(e):
        rcopy(G.at[e, 0:14], G.at[e, 0:14], rs.at[e], cr.at[e], sib, p).wait_send()
        rcopy(G.at[e, 0:16], G.at[e, 0:16], cs.at[e], cr.at[e], sib, p).wait_send()
        rcopy(img_h.at[e], G.at[e, s], xs.at[e], xr.at[e], xp, p).wait_send()
        sib_copy(e).wait_send()
        x_copy(e).wait_send()
        rcopy(G.at[e, 0:14], G.at[e, 0:14], brs.at[e], cr.at[e], sib, p).wait_send()
        all_halo(lambda copy: copy(e).wait_send(), False)


def whole_step(img, maps, meas, samp, wy, wz, w1, b1, w2, b2):
    sem = pltpu.SemaphoreType.DMA
    vm = pl.BlockSpec(memory_space=pltpu.VMEM)
    far = pl.BlockSpec(memory_space=pl.ANY)
    v = pltpu.VMEM
    return pl.pallas_call(
        kernel,
        out_shape=jax.ShapeDtypeStruct((E, 2, 2, 8, NY), BF),
        in_specs=[far] * 6 + [vm] * 3 + [pl.BlockSpec(memory_space=pltpu.SMEM)],
        out_specs=vm,
        scratch_shapes=[
            v((E, 2, 2, 8, NY), BF),
            v((E, SLABS, 2, 2, 8, NY), BF),
            v((SLABS, 2, 2, 8, NY), BF),
            v((E, 2, 2, NY, NZ), BF),
            v((E, NY, NZ), jnp.int32),
            v((2 * NY, 2 * NY), BF),
            v((2 * NZ, 2 * NZ), BF),
            v((E, 2, 8, 2, 2, 2, 8, NY), BF),
            v((E, 2, 8, 2, 2, 8, NY), BF),
            v((E, 2, 8, 2, 2, 8, NY), F32),
            v((4, 2, 2, E, 2, 2, 8, NY), BF),
            v((4, 2, 2, E, 2, 2, 8, NY), BF),
            v((E, 2, 2, 8, NY), BF),
            v((E, 2, 2, 8, NY), BF),
            v((NY, 2 * NZ), BF),
            v((2, E, 8, NY), F32),
            v((2, E, 8, NY), BF),
            v((2, 5, E, 8, NY), BF),
            v((5, E, 2, 2, 8, NY), BF),
            v((640, KA), BF),
            v((640, KB), BF),
            v((384, K2), BF),
            v((640, 1), F32),
            v((16, K2), F32),
            v((2, 16, NY), F32),
            v((15 * 128, 2 * NY), BF),
            v((15 * 32, 2 * NY), BF),
            v((3, 640, 2 * NY), F32),
            v((1920, 2 * NY), BF),
            v((6, 128, 128), F32),
            sem((E,)), sem((E,)),
            sem((E,)), sem((E, 2, 2, 4)),
            sem((E,)), sem((E,)),
            sem((4,)), sem((4,)),
            sem((2,)), sem((2, 4, 7)),
            sem((10,)),
            sem((E,)), sem((E,)),
            sem((E,)), sem((4, 2, 2, E)),
            sem((E,)), sem((E,)),
            sem((10, E)), sem((10, E)),
            sem((4, E)), sem((4, E)),
        ],
        compiler_params=pltpu.CompilerParams(
            collective_id=0, has_side_effects=True, vmem_limit_bytes=62 * 1024 * 1024
        ),
        name="whole_step",
    )(img, maps, meas, samp, wy, wz, w1, b1, w2, b2)


def on_device(
    current_image,
    coil_maps,
    measured,
    sampling,
    first_weight,
    first_bias,
    second_weight,
    second_bias,
):
    wy, wz = tables()
    out = whole_step(
        current_image[0], coil_maps, measured[0, 0], sampling[0],
        jnp.asarray(wy), jnp.asarray(wz), first_weight.reshape(FEAT, 270),
        first_bias[None], second_weight.reshape(10, 27 * FEAT), second_bias,
    )
    return out[None]


def solution(mesh):
    in_specs = (
        P("coil", None, None, None, "slab", None),
        P(None, None, None, "slab", None),
        P("coil", "slab", None, None, None, None, None),
        P("coil", None, None, None),
        P(),
        P(),
        P(),
        P(),
    )
    out_specs = P("coil", None, None, None, "slab", None)
    return jax.shard_map(
        on_device, mesh=mesh, in_specs=in_specs, out_specs=out_specs, check_vma=False
    )
```

```python
import functools
import math

import jax
import jax.numpy as jnp
import numpy as np
from jax import lax
from jax.experimental import pallas as pl
from jax.experimental.pallas import tpu as pltpu
from jax.sharding import PartitionSpec as P

MESH = pl.DeviceIdType.MESH
BF = jnp.bfloat16
F32 = jnp.float32
NY, NZ, E, FEAT = 384, 256, 5, 64
SLABS, PHASES = 32, 8
NT = (((1,), (1,)), ((), ()))
NN = (((1,), (0,)), ((), ()))
OFFSETS = (1, -1, 2, -2)
SHARE = (4, 1, 7, 3, 5, 2, 6)
KA, KB = 9 * 8 * 16, 9 * 2 * 16
K2 = 3 * 10 * FEAT


def dft_parts(length):
    indices = np.arange(length, dtype=np.int64)
    wrapped = indices[:, None] * indices[None, :] % length
    angles = wrapped.astype(np.float32) * np.float32(2.0 * math.pi / length)
    factor = np.float32(1.0 / math.sqrt(length))
    return np.cos(angles) * factor, np.sin(angles) * factor


def tables():
    cy, sy = dft_parts(NY)
    cz, sz = dft_parts(NZ)
    wy = np.stack([cy, sy]).astype(jnp.bfloat16)
    wz = np.stack([cz, sz]).astype(jnp.bfloat16)
    return wy, wz


def place():
    s = lax.axis_index("slab")
    p = lax.axis_index("coil")
    return s, p, s // 16, (s // 2) % 8, s % 2


def slab_of(xh, z, c):
    return xh * 16 + z * 2 + c


def rcopy(src, dst, ssem, rsem, s, p):
    return pltpu.make_async_remote_copy(
        src_ref=src,
        dst_ref=dst,
        send_sem=ssem,
        recv_sem=rsem,
        device_id={"slab": s, "coil": p},
        device_id_type=MESH,
    )


def mm(a, b, dims):
    return lax.dot_general(a, b, dims, preferred_element_type=F32)


STAGE = {1: ["m1"], 2: [("g", 0, 0, 1, 1)], 3: [("g", 0, 1, 1, 1)], 4: [("g", 0, 1, 1, 2)]}


Z_FIRST, X_FIRST = (3, 4), (0, 1, 2)


class Plan:
    LINKS = {"z0": (0.5, 2.1), "z1": (0.5, 2.1), "x": (0.5, 3.0), "c": (0.05, 1.6),
             "y": (2.2, 3.2), "e": (0.5, 6.0), "m1": (0.5, 4.0), "m2": (0.3, 3.0)}

    def __init__(self):
        self.tasks = []

    def add(self, name, fn, after=(), needs=(), sends=(), cost=0.05, rank=0):
        self.tasks.append((name, fn, tuple(after), tuple(needs), tuple(sends), cost, rank))

    def run(self):
        now, done, arrive, free = 0.0, {}, {}, {}
        left = list(self.tasks)
        while left:
            best = None
            for i, (name, _, after, needs, _, _, rank) in enumerate(left):
                if any(a not in done for a in after) or any(m not in arrive for m in needs):
                    continue
                ready = max([0.0] + [arrive[m] for m in needs])
                key = (max(ready, now), rank, i)
                if best is None or key < best[0]:
                    best = (key, i)
            name, fn, _, _, sends, cost, _ = left.pop(best[1])
            now = best[0][0] + cost
            for message, link, size in sends:
                rate, lag = self.LINKS[link]
                free[link] = max(free.get(link, 0.0), now) + rate * size
                arrive[message] = free[link] + lag
            done[name] = now
            fn()
        return now


def kernel(
    img_h, maps, meas_h, samp_h, wy_h, wz_h, w1_ref, b1_ref, w2_ref, b2_ref, out_ref,
    img, G, M, meas, samp, wy, wz, gd, sibbuf, S, rbuf, sbuf, xsb, xrb, xsb8, xrb8, res, esc, esend, erecv, U,
    W1A, W1B, W2, b1_s, w2_s, col_s, VA, VB, hacc, hid, osc,
    xs, xr, rs, rr, cs, cr, s1s, s1r, s2s, s2r, ls,
    bcs, bcr, brs, brr, bxs, bxr, es, er, us, ur,
):
    s, p, xh, z, c = place()
    sib = slab_of(xh, z, 1 - c)
    xp = slab_of(1 - xh, z, c)
    ring = [slab_of(xh, (z + 1) % 8, c), slab_of(xh, (z + 7) % 8, c)]
    has_up, has_down = s > 0, s < SLABS - 1

    def phase_there(q):
        return jnp.logical_and(p + q >= 0, p + q < PHASES)

    loads = [
        pltpu.make_async_copy(a, b, ls.at[i])
        for i, (a, b) in enumerate(
            (
                (img_h, img),
                (wy_h.at[0], wy.at[0:NY, 0:NY]),
                (wy_h.at[0], wy.at[NY:, NY:]),
                (wy_h.at[1], wy.at[0:NY, NY:]),
                (wz_h.at[0], wz.at[0:NZ, 0:NZ]),
                (wz_h.at[0], wz.at[NZ:, NZ:]),
                (wz_h.at[1], wz.at[NZ:, 0:NZ]),
                (samp_h, samp),
                (meas_h, meas),
            )
        )
    ]
    for load in loads:
        load.start()

    def weights1():
        k = lax.broadcasted_iota(jnp.int32, (270, 1), 0)
        source = ((k // 9 % 3 * 3 + k % 3) * 10 + k // 27) * 16 + k // 3 % 3
        for W, n, wide, first in ((W1A, KA, 8, 0), (W1B, KB, 2, 8)):
            padded = -(-n // 128) * 128
            m = lax.broadcasted_iota(jnp.int32, (1, padded), 1)
            target = (m // (16 * wide) * 10 + first + m // 16 % wide) * 16 + m % 16
            pick = jnp.where(source == target, 1.0, 0.0).astype(BF)
            base = mm(w1_ref[...], pick, NN)
            for zo in range(10):
                turned = base if zo == 0 else pltpu.roll(base, zo, 1)
                W[zo * FEAT : (zo + 1) * FEAT, :] = turned[:, :n].astype(BF)
        same = lax.broadcasted_iota(jnp.int32, (FEAT, FEAT), 0) == lax.broadcasted_iota(
            jnp.int32, (FEAT, FEAT), 1
        )
        bias = jnp.sum(jnp.where(same, b1_ref[...], 0.0), axis=1, keepdims=True)
        for zo in range(10):
            b1_s[zo * FEAT : (zo + 1) * FEAT, :] = bias
        col_s[...] = jnp.zeros_like(col_s)

    def weights2(d):
        k = lax.broadcasted_iota(jnp.int32, (27 * FEAT, 1), 0)
        source = jnp.where(k % 3 == d, k // 3 % 9 * FEAT + k // 27, -1)
        m = lax.broadcasted_iota(jnp.int32, (1, 640), 1)
        pick = jnp.where(source == m, 1.0, 0.0).astype(BF)
        base = mm(w2_ref[...], pick, NN)
        w2_s[...] = jnp.zeros_like(w2_s)
        for a in range(3):
            w2_s[0:10, a * 640 : a * 640 + 192] = base[:, a * 192 : a * 192 + 192]
        base = w2_s[...]
        for zz in range(8):
            turned = base if zz == 0 else pltpu.roll(base, zz * FEAT, 1)
            W2[pl.ds(pl.multiple_of(d * 128 + zz * 16, 16), 16), :] = turned.astype(BF)

    barrier = pltpu.get_barrier_semaphore()

    def greet(a, b):
        pl.semaphore_signal(
            barrier, inc=1, device_id={"slab": a, "coil": b}, device_id_type=MESH
        )

    for a in (sib, xp, ring[0], ring[1]):
        greet(a, p)
    for q in range(1, 8):
        greet(s, (p + q) % 8)
    for q in (-2, -1, 0, 1, 2):
        pl.when(jnp.logical_and(has_up, phase_there(q)))(lambda: greet(s - 1, p + q))
        pl.when(jnp.logical_and(has_down, phase_there(q)))(lambda: greet(s + 1, p + q))
    for j in range(4):
        delta = p + 8 * j

        @pl.when(delta != 0)
        def _():
            greet((s + 32 - delta) % 32, p)

    one = lambda cond: jnp.where(cond, 1, 0)
    aside = sum(one(phase_there(q)) for q in OFFSETS)
    pl.semaphore_wait(
        barrier, 15 - one(p == 0) + one(has_up) * (aside + 1) + one(has_down) * (aside + 1)
    )

    plan = Plan()

    def near(j):
        return (s + 32 - (p + 8 * j)) % 32

    def maps_first():
        for j in range(4):
            delta = p + 8 * j
            far = (s + delta) % 32

            @pl.when(delta != 0)
            def _():
                rcopy(maps.at[far], M.at[s], s1s.at[j], s1r.at[j], far, p).start()

            @pl.when(delta == 0)
            def _():
                pltpu.make_async_copy(maps.at[s], M.at[s], ls.at[9]).start()

    def maps_share(j):
        delta = p + 8 * j
        k = near(j)

        @pl.when(delta != 0)
        def _():
            rcopy(maps.at[s], M.at[k], s1s.at[j], s1r.at[j], k, p).wait_recv()

        @pl.when(delta == 0)
        def _():
            pltpu.make_async_copy(maps.at[s], M.at[s], ls.at[9]).wait()

        for q in SHARE:
            maps_copy(j, q, k, 0).start()

    def maps_copy(j, q, k, x):
        half = M.at[k, :, x]
        return rcopy(half, half, s2s.at[x], s2r.at[x, j, q - 1], s, (p + q) % 8)

    def maps_rest():
        for j in range(4):
            for q in SHARE:
                maps_copy(j, q, near(j), 1).start()

    def maps_wait(x):
        for q in SHARE:
            for j in range(4):
                k = (s + 32 - ((p + 8 - q) % 8 + 8 * j)) % 32
                maps_copy(j, q, k, x).wait_recv()

    plan.add("m1", maps_first, after=[("own", 0)],
             sends=[("m1a", "z0", 4), ("m1b", "z1", 4), ("m1", "m1", 4)], rank=-3)
    for j in range(4):
        plan.add(("m2", j), lambda j=j: maps_share(j), after=["m1"], needs=["m1", "m1a", "m1b"],
                 sends=[(("m2", j), "m2", 3.5), (("m2x", j), "x", 2)], rank=-1)
    plan.add("m2b", maps_rest, after=[("m2", j) for j in range(4)], sends=[("m2b", "m2", 14), ("m2bx", "x", 8)], rank=-1)

    def slot(col, dz):
        return slab_of((xh + col) % 2, (z + dz) % 8, c)

    def ring_copy(src, e, col, d, t, k):
        if t == 4:
            src, dst = src.at[d], G.at[e, k, d]
        else:
            dst = G.at[e, k]
        return rcopy(src, dst, rs.at[e], rr.at[e, col, d, t - 1], ring[d], p)

    def core_copy(src, e, k):
        return rcopy(src, G.at[e, k], cs.at[e], cr.at[e], sib, p)

    def own_start(e):
        for d in range(2):
            ring_copy(img_h.at[e], e, 0, d, 1, s).start()

    def own_aside():
        for e in range(E):
            rcopy(img_h.at[e], G.at[e, s], xs.at[e], xr.at[e], xp, p).start()
        for e in range(E):
            core_copy(img_h.at[e], e, s).start()
            G[e, s] = img[e]

    def cross(e):
        rcopy(img_h.at[e], G.at[e, xp], xs.at[e], xr.at[e], xp, p).wait_recv()
        for d in range(2):
            ring_copy(G.at[e, xp], e, 1, d, 1, xp).start()
        core_copy(G.at[e, xp], e, xp).start()

    def spread(e, k):
        core_copy(G.at[e, k], e, k).start()
        if e in Z_FIRST:
            rcopy(G.at[e, k], G.at[e, k], xs.at[e], xr.at[e], xp, p).start()

    def hop(e, col, d, t):
        k = slot(col, (8 - t) if d == 0 else t)
        ring_copy(G.at[e, k], e, col, d, t, k).wait_recv()
        if t < 4:
            ring_copy(G.at[e, k], e, col, d, t + 1, k).start()
            spread(e, k)

    def far_slab(e, col):
        for d in range(2):
            hop(e, col, d, 4)
        spread(e, slot(col, 4))

    def cross_all(e):
        rcopy(G.at[e, 0:8], G.at[e, 0:8], xs.at[e], xr.at[e], xp, p).wait_recv()

        @pl.loop(0, 8)
        def _(zz):
            k = slab_of(1 - xh, zz, c)
            core_copy(G.at[e, k], e, k).start()

    def gathered(e):
        rcopy(G.at[e, 0:16], G.at[e, 0:16], cs.at[e], cr.at[e], sib, p).wait_recv()

    plan.add("img", lambda: loads[0].wait(), cost=0.3, rank=-2)
    plan.add("aside", own_aside, after=["m1", "img"], sends=[(("x", e), "x", 1) for e in range(E)], rank=-2)
    for e in range(E):
        plan.add(("own", e), lambda e=e: own_start(e), after=["img"] + STAGE.get(e, []),
                 sends=[(("g", e, 0, 0, 1), "z0", 1), (("g", e, 0, 1, 1), "z1", 1)],
                 rank=-2 if e < 1 else e)
        direct = e in Z_FIRST
        if direct:
            xneeds = [("xg", e, t, d) for t in range(1, 4) for d in range(2)] + [("xg", e, 4)]
            plan.add(("cross", e), lambda e=e: cross_all(e), needs=xneeds, after=[("far", e, 0)],
                     sends=[(("far", e, 1), "c", 8)], rank=e)
        else:
            plan.add(("cross", e), lambda e=e: cross(e), after=[("own", e)], needs=[("x", e)],
                     sends=[(("g", e, 1, 0, 1), "z0", 1), (("g", e, 1, 1, 1), "z1", 1)], rank=e)
        for col in range(1 if direct else 2):
            for t in range(1, 4):
                for d in range(2):
                    m = ("g", e, col, d, t)
                    plan.add(m, lambda e=e, col=col, d=d, t=t: hop(e, col, d, t), needs=[m],
                             sends=[(("g", e, col, d, t + 1), "z%d" % d, 0.5 if t == 3 else 1)]
                             + [(("xg", e, t, d), "x", 1)] * direct, rank=e)
            plan.add(("far", e, col), lambda e=e, col=col: far_slab(e, col),
                     after=[("g", e, k, d, t) for k in range(col + 1) for d in range(2) for t in range(1, 4)],
                     needs=[("g", e, col, 0, 4), ("g", e, col, 1, 4)],
                     sends=[(("far", e, col), "c", 1)] + [(("xg", e, 4), "x", 1)] * direct, rank=e)
        plan.add(("full", e), lambda e=e: gathered(e), after=[("far", e, 0), ("cross" if direct else "far", e, 1)[: 3 - direct]],
                 needs=[("far", e, 0), ("far", e, 1)], rank=e)

    def tables_wait():
        for load in loads[1:]:
            load.wait()
        wy[NY:, 0:NY] = -wy[0:NY, NY:]
        wz[0:NZ, NZ:] = -wz[NZ:, 0:NZ]
        maps_wait(0)

    plan.add("tables", tables_wait, after=[("m2", j) for j in range(4)],
             needs=[("m2", j) for j in range(4)], rank=0)

    plan.add("maps1", lambda: maps_wait(1), needs=["m2b"], after=["tables"], rank=0)
    plan.add("w1", weights1, after=[("own", 1)], cost=2.0, rank=6)
    plan.add("w2", lambda: pl.loop(0, 3)(weights2), after=["w1"], cost=1.6, rank=7)

    def block(e, x):
        mask = samp[e].astype(F32)
        wide = lambda v: v.astype(F32).reshape(NZ, NY)
        mr, mi = wide(M[:, 0, x]), wide(M[:, 1, x])
        ir, ii = wide(G[e, :, 0, x]), wide(G[e, :, 1, x])
        pr = (mr * ir - mi * ii).astype(BF)
        pi = (mr * ii + mi * ir).astype(BF)
        r = mm(wy[...], jnp.concatenate([pr, pi], axis=1), NT).astype(BF)
        rc = jnp.concatenate([r[:NY], r[NY:]], axis=1)
        sp = mm(rc, wz[...], NN)
        dr = (mask * (sp[:, :NZ] - meas[e, 0, x].astype(F32))).astype(BF)
        di = (mask * (sp[:, NZ:] - meas[e, 1, x].astype(F32))).astype(BF)
        res[:, :NZ] = dr
        res[:, NZ:] = di

    def block_back(e, x):
        wide = lambda v: v.astype(F32).reshape(NZ, NY)
        mr, mi = wide(M[:, 0, x]), wide(M[:, 1, x])
        b = mm(wz[...], res[...], NT).astype(BF)
        bc = jnp.concatenate([b[:NZ], b[NZ:]], axis=1)
        im = mm(bc, wy[...], NN)
        br, bi = im[:, :NY], im[:, NY:]
        cells = (2, 8, 2, 8, NY)
        gd[e, :, :, :, 0, x] = (mr * br + mi * bi).reshape(cells).astype(BF)
        gd[e, :, :, :, 1, x] = (mr * bi - mi * br).reshape(cells).astype(BF)

    def sib_copy(e):
        return rcopy(gd.at[e, :, :, 1 - c], sibbuf.at[e], bcs.at[e], bcr.at[e], sib, p)

    def last_block(e):
        block_back(e, 1)
        sib_copy(e).start()

    def back_copy(h, e, col, d):
        src, dst = sbuf.at[h, col, d, e], rbuf.at[h, col, d, e]
        if h == 0:
            src, dst = src.at[d], dst.at[d]
        return rcopy(src, dst, brs.at[e], brr.at[h, col, d, e], ring[d], p)

    def x_copy(e):
        return rcopy(xsb.at[e], xrb.at[e], bxs.at[e], bxr.at[e], xp, p)

    def pair_sum(e):
        sib_copy(e).wait_recv()
        S[e] = gd[e, :, :, c].astype(F32) + sibbuf[e].astype(F32)
        if e in X_FIRST:
            xsb8[e] = S[e, 1 - xh].astype(BF)
            x_copy8(e).start()
        else:
            first_hop(e, (1, 0))

    def first_hop(e, cols):
        for col in cols:
            for d in range(2):
                sbuf[0, col, d, e, d] = S[e, (xh + col) % 2, (z + 4) % 8, d].astype(BF)
                back_copy(0, e, col, d).start()

    def x_copy8(e):
        return rcopy(xsb8.at[e], xrb8.at[e], bxs.at[e], bxr.at[e], xp, p)

    def x_sum(e):
        x_copy8(e).wait_recv()
        S[e, xh] = S[e, xh] + xrb8[e].astype(F32)
        first_hop(e, (0,))

    def back_hop(e, h, col):
        for d in range(2):
            back_copy(h - 1, e, col, d).wait_recv()
            k = 4 - h
            tz = (z + k) % 8 if d == 0 else (z + 8 - k) % 8
            lane = (xh + col) % 2
            if h == 1:
                v = S[e, lane, tz, d] + rbuf[0, col, d, e, d].astype(F32)
                sbuf[1, col, d, e, d] = v.astype(BF)
                sbuf[1, col, d, e, 1 - d] = S[e, lane, tz, 1 - d].astype(BF)
            else:
                v = S[e, lane, tz] + rbuf[h - 1, col, d, e].astype(F32)
                sbuf[h, col, d, e] = v.astype(BF)
            back_copy(h, e, col, d).start()

    def back_end(e, col):
        for d in range(2):
            back_copy(3, e, col, d).wait_recv()
        lane = (xh + col) % 2
        v = S[e, lane, z] + rbuf[3, col, 0, e].astype(F32) + rbuf[3, col, 1, e].astype(F32)
        if col == 1:
            xsb[e] = v.astype(BF)
            x_copy(e).start()
        else:
            S[e, lane, z] = v

    def u_copy(i, e):
        q = OFFSETS[i]
        return rcopy(U.at[2, e], U.at[2 - q, e], us.at[i, e], ur.at[i, e], s, p + q)

    def e_copy(i, q, e):
        k = 5 * i + q + 2
        return rcopy(esend.at[i, e], erecv.at[i, 2 - q, e], es.at[k, e], er.at[k, e], (s + 1, s - 1)[i], p + q)

    def all_halo(act, inward):
        for i, q in enumerate(OFFSETS):
            pl.when(phase_there(-q if inward else q))(lambda: act(lambda e: u_copy(i, e)))
        for i, cond in enumerate((has_up, has_down) if inward else (has_down, has_up)):
            for q in (0, -1, 1, -2, 2):
                both = jnp.logical_and(cond, phase_there(-q if inward else q))
                pl.when(both)(lambda: act(lambda e: e_copy(i, q, e)))

    def update(e):
        g = S[e, xh, z]
        if e not in X_FIRST:
            x_copy(e).wait_recv()
            g = g + xrb[e].astype(F32)
        u = (img[e].astype(F32) - g).astype(BF)
        U[2, e] = u
        v = u.astype(F32)
        for i, first in enumerate((6, 0)):
            for r in range(2):
                for x in range(2):
                    k = 4 * r + 2 * x
                    esc[i, e, k : k + 2] = v[r, x, first : first + 2]
            esend[i, e] = esc[i, e].astype(BF)
        all_halo(lambda copy: copy(e).start(), False)

    lane = lax.broadcasted_iota(jnp.int32, (32, NY), 1)

    def columns(e):
        all_halo(lambda copy: copy(e).wait_recv(), True)
        V, rows, part0 = (VB, 32, 0) if isinstance(e, int) else (VA, 128, e * 32)

        @pl.loop(0, 5)
        def _(q):
            there = jnp.logical_and(p + q >= 2, p + q < PHASES + 2)
            up = jnp.where(has_up, erecv[0, q, e].astype(F32), 0.0)
            down = jnp.where(has_down, erecv[1, q, e].astype(F32), 0.0)
            for x in range(2):
                col_s[:, 2:10] = U[q, e, :, x].astype(F32)
                for r in range(2):
                    k = 4 * r + 2 * x
                    col_s[r, 0:2] = up[k : k + 2]
                    col_s[r, 10:12] = down[k : k + 2]
                v = jnp.where(there, col_s[...].reshape(32, NY), 0.0)
                back = jnp.where(lane == 0, 0.0, pltpu.roll(v, 1, 1))
                ahead = jnp.where(lane == NY - 1, 0.0, pltpu.roll(v, NY - 1, 1))
                for d, part in enumerate((back, v, ahead)):
                    first = pl.multiple_of((q * 3 + d) * rows + part0, 32)
                    V[pl.ds(first, 32), x * NY : (x + 1) * NY] = part.astype(BF)

    def conv_part(t):
        cells = VA[pl.ds(pl.multiple_of(t * 384, 384), KA), :]
        hacc[t] = mm(W1A[...], cells, NN) + b1_s[...]

    before = []
    later = ["maps1"]
    for e in range(E):
        for x in range(2):
            plan.add(("dft", e, x), lambda e=e, x=x: block(e, x), after=["tables", ("full", e)] + before + later * x,
                     cost=0.93, rank=20 + e)
            before = [("back", e, x)]
            plan.add(before[0], lambda e=e, x=x: last_block(e) if x else block_back(e, 0),
                     after=[("dft", e, x)], cost=0.93, sends=[(("bc", e), "c", 16)] * x, rank=20 + e)
        cols = (0,) if e in X_FIRST else (1, 0)
        starts = [(("b", e, col, 0), "z%d" % d, 0.5) for col in cols for d in range(2)]
        if e in X_FIRST:
            plan.add(("pair", e), lambda e=e: pair_sum(e), after=[("back", e, 1)], needs=[("bc", e)], cost=0.25,
                     sends=[(("bx", e), "x", 8)], rank=10 + e)
            plan.add(("xsum", e), lambda e=e: x_sum(e), after=[("pair", e)], needs=[("bx", e)], cost=0.15,
                     sends=starts, rank=10 + e)
        else:
            plan.add(("pair", e), lambda e=e: pair_sum(e), after=[("back", e, 1)], needs=[("bc", e)], cost=0.25,
                     sends=starts, rank=10 + e)
        for h in range(1, 4):
            for col in cols:
                plan.add(("back", e, h, col), lambda e=e, h=h, col=col: back_hop(e, h, col),
                         needs=[("b", e, col, h - 1)], after=[("pair", e)] + [("back", e, h, 1)] * ((1 - col) * (len(cols) - 1)),
                         sends=[(("b", e, col, h), "z%d" % d, 1) for d in range(2)], cost=0.03, rank=10 + e)
        for col in cols:
            plan.add(("end", e, col), lambda e=e, col=col: back_end(e, col), needs=[("b", e, col, 3)],
                     after=[("back", e, 3, col)], sends=[(("bx", e), "x", 1)] * col, cost=0.1, rank=10 + e)
        plan.add(("upd", e), lambda e=e: update(e), needs=[("bx", e)], after=[("end", e, 0)], cost=0.05,
                 sends=[(("e", e), "e", 1), (("u", e), "y", 1)], rank=10 + e)
    plan.add("cols", lambda: pl.loop(0, 4)(columns), needs=[(k, 3) for k in "ue"], after=[("upd", 4)], cost=1.0)
    plan.add("conv", lambda: pl.loop(0, 3)(conv_part), after=["cols"], cost=5.6, rank=30)
    plan.add("cols4", lambda: columns(4), needs=[(k, 4) for k in "ue"], after=["cols"], cost=0.25, rank=40)

    plan.run()

    rows = lax.broadcasted_iota(jnp.int32, (640, 2 * NY), 0)
    lowest = jnp.where(s == 0, FEAT, 0)
    highest = jnp.where(s == SLABS - 1, 9 * FEAT, 10 * FEAT)

    @pl.loop(0, 3)
    def _(t):
        there = jnp.logical_and(p + t >= 1, p + t < PHASES + 1)
        cells = VB[pl.ds(pl.multiple_of(t * 96, 96), KB), :]
        h = mm(W1B[...], cells, NN) + hacc[t]
        keep = jnp.logical_and(jnp.logical_and(rows >= lowest, rows < highest), there)
        first = pl.multiple_of(t * 640, 640)
        hid[pl.ds(first, 640), :] = jnp.where(keep, jnp.maximum(h, 0.0), 0.0).astype(BF)

    o = mm(W2[...], hid[...], NN)
    lane2 = lax.broadcasted_iota(jnp.int32, (128, 2 * NY), 1) % NY
    total = (
        o[128:256]
        + jnp.where(lane2 == 0, 0.0, pltpu.roll(o[:128], 1, 1))
        + jnp.where(lane2 == NY - 1, 0.0, pltpu.roll(o[256:], 2 * NY - 1, 1))
    )
    for k in range(6):
        osc[k] = total[:, k * 128 : (k + 1) * 128]
    for i in range(10):
        for x in range(2):
            second = jnp.concatenate(
                [osc[3 * x + k, pl.ds(i, 8, stride=16), :] for k in range(3)], axis=1
            )
            v = U[2, i // 2, i % 2, x].astype(F32) + second + b2_ref[i]
            out_ref[i // 2, i % 2, x] = v.astype(BF)

    for j in range(4):
        delta = p + 8 * j
        far = (s + delta) % 32

        @pl.when(delta != 0)
        def _():
            rcopy(maps.at[far], M.at[s], s1s.at[j], s1r.at[j], far, p).wait_send()

    for x in range(2):
        rcopy(G.at[0, 0:14], G.at[0, 0:14], s2s.at[x], s2r.at[0, 0, 0], s, p).wait_send()

    def left(e, n, sem):
        rcopy(G.at[e, 0:n], G.at[e, 0:n], sem.at[e], cr.at[e], sib, p).wait_send()

    for e in range(E):
        left(e, 7 if e in Z_FIRST else 14, rs)
        left(e, 8 if e in Z_FIRST else 1, xs)
        left(e, 7 if e in X_FIRST else 14, brs)
        left(e, 8 if e in X_FIRST else 1, bxs)

    @pl.loop(0, E)
    def _(e):
        left(e, 16, cs)
        sib_copy(e).wait_send()
        all_halo(lambda copy: copy(e).wait_send(), False)


def whole_step(img, maps, meas, samp, wy, wz, w1, b1, w2, b2):
    sem = pltpu.SemaphoreType.DMA
    vm = pl.BlockSpec(memory_space=pltpu.VMEM)
    far = pl.BlockSpec(memory_space=pl.ANY)
    v = pltpu.VMEM
    return pl.pallas_call(
        kernel,
        out_shape=jax.ShapeDtypeStruct((E, 2, 2, 8, NY), BF),
        in_specs=[far] * 6 + [vm] * 3 + [pl.BlockSpec(memory_space=pltpu.SMEM)],
        out_specs=vm,
        scratch_shapes=[
            v((E, 2, 2, 8, NY), BF),
            v((E, SLABS, 2, 2, 8, NY), BF),
            v((SLABS, 2, 2, 8, NY), BF),
            v((E, 2, 2, NY, NZ), BF),
            v((E, NY, NZ), jnp.int32),
            v((2 * NY, 2 * NY), BF),
            v((2 * NZ, 2 * NZ), BF),
            v((E, 2, 8, 2, 2, 2, 8, NY), BF),
            v((E, 2, 8, 2, 2, 8, NY), BF),
            v((E, 2, 8, 2, 2, 8, NY), F32),
            v((4, 2, 2, E, 2, 2, 8, NY), BF),
            v((4, 2, 2, E, 2, 2, 8, NY), BF),
            v((E, 2, 2, 8, NY), BF),
            v((E, 2, 2, 8, NY), BF),
            v((3, 8, 2, 2, 8, NY), BF),
            v((3, 8, 2, 2, 8, NY), BF),
            v((NY, 2 * NZ), BF),
            v((2, E, 8, NY), F32),
            v((2, E, 8, NY), BF),
            v((2, 5, E, 8, NY), BF),
            v((5, E, 2, 2, 8, NY), BF),
            v((640, KA), BF),
            v((640, KB), BF),
            v((384, K2), BF),
            v((640, 1), F32),
            v((16, K2), F32),
            v((2, 16, NY), F32),
            v((15 * 128, 2 * NY), BF),
            v((15 * 32, 2 * NY), BF),
            v((3, 640, 2 * NY), F32),
            v((1920, 2 * NY), BF),
            v((6, 128, 128), F32),
            sem((E,)), sem((E,)),
            sem((E,)), sem((E, 2, 2, 4)),
            sem((E,)), sem((E,)),
            sem((4,)), sem((4,)),
            sem((2,)), sem((2, 4, 7)),
            sem((10,)),
            sem((E,)), sem((E,)),
            sem((E,)), sem((4, 2, 2, E)),
            sem((E,)), sem((E,)),
            sem((10, E)), sem((10, E)),
            sem((4, E)), sem((4, E)),
        ],
        compiler_params=pltpu.CompilerParams(
            collective_id=0, has_side_effects=True, vmem_limit_bytes=62 * 1024 * 1024
        ),
        name="whole_step",
    )(img, maps, meas, samp, wy, wz, w1, b1, w2, b2)


def on_device(
    current_image,
    coil_maps,
    measured,
    sampling,
    first_weight,
    first_bias,
    second_weight,
    second_bias,
):
    wy, wz = tables()
    out = whole_step(
        current_image[0], coil_maps, measured[0, 0], sampling[0],
        jnp.asarray(wy), jnp.asarray(wz), first_weight.reshape(FEAT, 270),
        first_bias[None], second_weight.reshape(10, 27 * FEAT), second_bias,
    )
    return out[None]


def solution(mesh):
    in_specs = (
        P("coil", None, None, None, "slab", None),
        P(None, None, None, "slab", None),
        P("coil", "slab", None, None, None, None, None),
        P("coil", None, None, None),
        P(),
        P(),
        P(),
        P(),
    )
    out_specs = P("coil", None, None, None, "slab", None)
    return jax.shard_map(
        on_device, mesh=mesh, in_specs=in_specs, out_specs=out_specs, check_vma=False
    )
```

```python
import functools
import math

import jax
import jax.numpy as jnp
import numpy as np
from jax import lax
from jax.experimental import pallas as pl
from jax.experimental.pallas import tpu as pltpu
from jax.sharding import PartitionSpec as P

MESH = pl.DeviceIdType.MESH
BF = jnp.bfloat16
F32 = jnp.float32
NY, NZ, E, FEAT = 384, 256, 5, 64
SLABS, PHASES = 32, 8
NT = (((1,), (1,)), ((), ()))
NN = (((1,), (0,)), ((), ()))
TN = (((0,), (0,)), ((), ()))
OFFSETS = (2, -2, 1, -1)
SHARE = (4, 1, 7, 3, 5, 2, 6)
KA, KB = 9 * 8 * 16, 9 * 2 * 16
K2 = 3 * 10 * FEAT


def dft_parts(length):
    indices = np.arange(length, dtype=np.int64)
    wrapped = indices[:, None] * indices[None, :] % length
    angles = wrapped.astype(np.float32) * np.float32(2.0 * math.pi / length)
    factor = np.float32(1.0 / math.sqrt(length))
    return np.cos(angles) * factor, np.sin(angles) * factor


def tables():
    cy, sy = dft_parts(NY)
    cz, sz = dft_parts(NZ)
    wy = np.stack([cy, sy]).astype(jnp.bfloat16)
    wz = np.stack([cz, sz]).astype(jnp.bfloat16)
    return wy, wz


def place():
    s = lax.axis_index("slab")
    p = lax.axis_index("coil")
    return s, p, s // 16, (s // 2) % 8, s % 2


def slab_of(xh, z, c):
    return xh * 16 + z * 2 + c


def rcopy(src, dst, ssem, rsem, s, p):
    return pltpu.make_async_remote_copy(
        src_ref=src,
        dst_ref=dst,
        send_sem=ssem,
        recv_sem=rsem,
        device_id={"slab": s, "coil": p},
        device_id_type=MESH,
    )


def mm(a, b, dims):
    return lax.dot_general(a, b, dims, preferred_element_type=F32)


STAGE = {1: ["m1"], 2: [("g", 0, 0, 1, 1)], 3: [("g", 0, 1, 1, 1)], 4: [("g", 0, 1, 1, 2)]}


Z_FIRST, X_FIRST = (3, 4), (0, 1, 2)


class Plan:
    LINKS = {"z0": (0.5, 2.1), "z1": (0.5, 2.1), "x": (0.5, 3.0), "c": (0.05, 1.6),
             "y": (2.2, 3.2), "e": (0.5, 6.0), "m1": (0.5, 4.0), "m2": (0.3, 3.0)}

    def __init__(self):
        self.tasks = []

    def add(self, name, fn, after=(), needs=(), sends=(), cost=0.05, rank=0):
        self.tasks.append((name, fn, tuple(after), tuple(needs), tuple(sends), cost, rank))

    def run(self):
        now, done, arrive, free = 0.0, {}, {}, {}
        left = list(self.tasks)
        while left:
            best = None
            for i, (name, _, after, needs, _, _, rank) in enumerate(left):
                if any(a not in done for a in after) or any(m not in arrive for m in needs):
                    continue
                ready = max([0.0] + [arrive[m] for m in needs])
                key = (max(ready, now), rank, i)
                if best is None or key < best[0]:
                    best = (key, i)
            name, fn, _, _, sends, cost, _ = left.pop(best[1])
            now = best[0][0] + cost
            for message, link, size in sends:
                rate, lag = self.LINKS[link]
                free[link] = max(free.get(link, 0.0), now) + rate * size
                arrive[message] = free[link] + lag
            done[name] = now
            fn()
        return now


def kernel(
    img_h, maps, meas_h, samp_h, wy_h, wz_h, w1_h, b1_ref, w2_h, b2_ref, out_ref,
    img, G, M, meas, samp, wy, wz, gd, sibbuf, S, rbuf, sbuf, xsb, xrb, xsb8, xrb8, res, esc, esend, erecv, U,
    w1_ref, w2_ref, W1A, W1B, W2, b1_s, w2_s, col_s, VA, VB, hacc, hid, osc,
    xs, xr, rs, rr, cs, cr, s1s, s1r, s2s, s2r, ls,
    bcs, bcr, brs, brr, bxs, bxr, es, er, us, ur,
):
    s, p, xh, z, c = place()
    sib = slab_of(xh, z, 1 - c)
    xp = slab_of(1 - xh, z, c)
    ring = [slab_of(xh, (z + 1) % 8, c), slab_of(xh, (z + 7) % 8, c)]
    has_up, has_down = s > 0, s < SLABS - 1

    def phase_there(q):
        return jnp.logical_and(p + q >= 0, p + q < PHASES)

    loads = [
        pltpu.make_async_copy(a, b, ls.at[i])
        for i, (a, b) in enumerate(
            (
                (img_h, img),
                (wy_h.at[0], wy.at[0:NY, 0:NY]),
                (wy_h.at[0], wy.at[NY:, NY:]),
                (wy_h.at[1], wy.at[0:NY, NY:]),
                (wz_h.at[0], wz.at[0:NZ, 0:NZ]),
                (wz_h.at[0], wz.at[NZ:, NZ:]),
                (wz_h.at[1], wz.at[NZ:, 0:NZ]),
                (samp_h, samp),
                (meas_h, meas),
                (w1_h, w1_ref),
                (w2_h, w2_ref),
            )
        )
    ]
    for load in loads:
        load.start()

    def weights1():
        for load in loads[9:]:
            load.wait()
        k = lax.broadcasted_iota(jnp.int32, (270, 1), 0)
        source = ((k // 9 % 3 * 3 + k % 3) * 10 + k // 27) * 16 + k // 3 % 3
        for W, n, wide, first in ((W1A, KA, 8, 0), (W1B, KB, 2, 8)):
            padded = -(-n // 128) * 128
            m = lax.broadcasted_iota(jnp.int32, (1, padded), 1)
            target = (m // (16 * wide) * 10 + first + m // 16 % wide) * 16 + m % 16
            pick = jnp.where(source == target, 1.0, 0.0).astype(BF)
            base = mm(w1_ref[...], pick, TN)
            for zo in range(10):
                turned = base if zo == 0 else pltpu.roll(base, zo, 1)
                W[zo * FEAT : (zo + 1) * FEAT, :] = turned[:, :n].astype(BF)
        same = lax.broadcasted_iota(jnp.int32, (FEAT, FEAT), 0) == lax.broadcasted_iota(
            jnp.int32, (FEAT, FEAT), 1
        )
        bias = jnp.sum(jnp.where(same, b1_ref[...], 0.0), axis=1, keepdims=True)
        for zo in range(10):
            b1_s[zo * FEAT : (zo + 1) * FEAT, :] = bias
        col_s[...] = jnp.zeros_like(col_s)

    def weights2(d):
        k = lax.broadcasted_iota(jnp.int32, (27 * FEAT, 1), 0)
        source = jnp.where(k % 3 == d, k // 3 % 9 * FEAT + k // 27, -1)
        m = lax.broadcasted_iota(jnp.int32, (1, 640), 1)
        pick = jnp.where(source == m, 1.0, 0.0).astype(BF)
        base = mm(w2_ref[...], pick, TN)
        w2_s[...] = jnp.zeros_like(w2_s)
        for a in range(3):
            w2_s[0:10, a * 640 : a * 640 + 192] = base[:, a * 192 : a * 192 + 192]
        base = w2_s[...]
        for zz in range(8):
            turned = base if zz == 0 else pltpu.roll(base, zz * FEAT, 1)
            W2[pl.ds(pl.multiple_of(d * 128 + zz * 16, 16), 16), :] = turned.astype(BF)

    barrier = pltpu.get_barrier_semaphore()

    def greet(a, b):
        pl.semaphore_signal(
            barrier, inc=1, device_id={"slab": a, "coil": b}, device_id_type=MESH
        )

    for a in (sib, xp, ring[0], ring[1]):
        greet(a, p)
    for q in range(1, 8):
        greet(s, (p + q) % 8)
    for q in (-2, -1, 0, 1, 2):
        pl.when(jnp.logical_and(has_up, phase_there(q)))(lambda: greet(s - 1, p + q))
        pl.when(jnp.logical_and(has_down, phase_there(q)))(lambda: greet(s + 1, p + q))
    for j in range(4):
        delta = p + 8 * j

        @pl.when(delta != 0)
        def _():
            greet((s + 32 - delta) % 32, p)

    one = lambda cond: jnp.where(cond, 1, 0)
    aside = sum(one(phase_there(q)) for q in OFFSETS)
    pl.semaphore_wait(
        barrier, 15 - one(p == 0) + one(has_up) * (aside + 1) + one(has_down) * (aside + 1)
    )

    plan = Plan()

    def near(j):
        return (s + 32 - (p + 8 * j)) % 32

    def maps_first():
        for j in range(4):
            delta = p + 8 * j
            far = (s + delta) % 32

            @pl.when(delta != 0)
            def _():
                rcopy(maps.at[far], M.at[s], s1s.at[j], s1r.at[j], far, p).start()

            @pl.when(delta == 0)
            def _():
                pltpu.make_async_copy(maps.at[s], M.at[s], ls.at[11]).start()

    def maps_share(j):
        delta = p + 8 * j
        k = near(j)

        @pl.when(delta != 0)
        def _():
            rcopy(maps.at[s], M.at[k], s1s.at[j], s1r.at[j], k, p).wait_recv()

        @pl.when(delta == 0)
        def _():
            pltpu.make_async_copy(maps.at[s], M.at[s], ls.at[11]).wait()

        for q in SHARE:
            maps_copy(j, q, k, 0).start()

    def maps_copy(j, q, k, x):
        half = M.at[k, :, x]
        return rcopy(half, half, s2s.at[x], s2r.at[x, j, q - 1], s, (p + q) % 8)

    def maps_rest():
        for j in range(4):
            for q in SHARE:
                maps_copy(j, q, near(j), 1).start()

    def maps_wait(x):
        for q in SHARE:
            for j in range(4):
                k = (s + 32 - ((p + 8 - q) % 8 + 8 * j)) % 32
                maps_copy(j, q, k, x).wait_recv()

    plan.add("m1", maps_first, after=[("own", 0)],
             sends=[("m1a", "z0", 4), ("m1b", "z1", 4), ("m1", "m1", 4)], rank=-3)
    for j in range(4):
        plan.add(("m2", j), lambda j=j: maps_share(j), after=["m1"], needs=["m1", "m1a", "m1b"],
                 sends=[(("m2", j), "m2", 3.5), (("m2x", j), "x", 2)], rank=-1)
    plan.add("m2b", maps_rest, after=[("m2", j) for j in range(4)], sends=[("m2b", "m2", 14), ("m2bx", "x", 8)], rank=-1)

    def slot(col, dz):
        return slab_of((xh + col) % 2, (z + dz) % 8, c)

    def ring_copy(src, e, col, d, t, k):
        if t == 4:
            src, dst = src.at[d], G.at[e, k, d]
        else:
            dst = G.at[e, k]
        return rcopy(src, dst, rs.at[e], rr.at[e, col, d, t - 1], ring[d], p)

    def core_copy(src, e, k):
        return rcopy(src, G.at[e, k], cs.at[e], cr.at[e], sib, p)

    def own_start(e):
        for d in range(2):
            ring_copy(img_h.at[e], e, 0, d, 1, s).start()

    def own_aside():
        for e in range(E):
            rcopy(img_h.at[e], G.at[e, s], xs.at[e], xr.at[e], xp, p).start()
        for e in range(E):
            core_copy(img_h.at[e], e, s).start()
            G[e, s] = img[e]

    def cross(e):
        rcopy(img_h.at[e], G.at[e, xp], xs.at[e], xr.at[e], xp, p).wait_recv()
        for d in range(2):
            ring_copy(G.at[e, xp], e, 1, d, 1, xp).start()
        core_copy(G.at[e, xp], e, xp).start()

    def spread(e, k):
        core_copy(G.at[e, k], e, k).start()
        if e in Z_FIRST:
            rcopy(G.at[e, k], G.at[e, k], xs.at[e], xr.at[e], xp, p).start()

    def hop(e, col, d, t):
        k = slot(col, (8 - t) if d == 0 else t)
        ring_copy(G.at[e, k], e, col, d, t, k).wait_recv()
        if t < 4:
            ring_copy(G.at[e, k], e, col, d, t + 1, k).start()
            spread(e, k)

    def far_slab(e, col):
        for d in range(2):
            hop(e, col, d, 4)
        spread(e, slot(col, 4))

    def cross_all(e):
        rcopy(G.at[e, 0:8], G.at[e, 0:8], xs.at[e], xr.at[e], xp, p).wait_recv()

        @pl.loop(0, 8)
        def _(zz):
            k = slab_of(1 - xh, zz, c)
            core_copy(G.at[e, k], e, k).start()

    def gathered(e):
        rcopy(G.at[e, 0:16], G.at[e, 0:16], cs.at[e], cr.at[e], sib, p).wait_recv()

    plan.add("img", lambda: loads[0].wait(), cost=0.3, rank=-2)
    plan.add("aside", own_aside, after=["m1", "img"], sends=[(("x", e), "x", 1) for e in range(E)], rank=-2)
    for e in range(E):
        plan.add(("own", e), lambda e=e: own_start(e), after=["img"] + STAGE.get(e, []),
                 sends=[(("g", e, 0, 0, 1), "z0", 1), (("g", e, 0, 1, 1), "z1", 1)],
                 rank=-2 if e < 1 else e)
        direct = e in Z_FIRST
        if direct:
            xneeds = [("xg", e, t, d) for t in range(1, 4) for d in range(2)] + [("xg", e, 4)]
            plan.add(("cross", e), lambda e=e: cross_all(e), needs=xneeds, after=[("far", e, 0)],
                     sends=[(("far", e, 1), "c", 8)], rank=e)
        else:
            plan.add(("cross", e), lambda e=e: cross(e), after=[("own", e)], needs=[("x", e)],
                     sends=[(("g", e, 1, 0, 1), "z0", 1), (("g", e, 1, 1, 1), "z1", 1)], rank=e)
        for col in range(1 if direct else 2):
            for t in range(1, 4):
                for d in range(2):
                    m = ("g", e, col, d, t)
                    plan.add(m, lambda e=e, col=col, d=d, t=t: hop(e, col, d, t), needs=[m],
                             sends=[(("g", e, col, d, t + 1), "z%d" % d, 0.5 if t == 3 else 1)]
                             + [(("xg", e, t, d), "x", 1)] * direct, rank=e)
            plan.add(("far", e, col), lambda e=e, col=col: far_slab(e, col),
                     after=[("g", e, k, d, t) for k in range(col + 1) for d in range(2) for t in range(1, 4)],
                     needs=[("g", e, col, 0, 4), ("g", e, col, 1, 4)],
                     sends=[(("far", e, col), "c", 1)] + [(("xg", e, 4), "x", 1)] * direct, rank=e)
        plan.add(("full", e), lambda e=e: gathered(e), after=[("far", e, 0), ("cross" if direct else "far", e, 1)[: 3 - direct]],
                 needs=[("far", e, 0), ("far", e, 1)], rank=e)

    def tables_wait():
        for load in loads[1:9]:
            load.wait()
        wy[NY:, 0:NY] = -wy[0:NY, NY:]
        wz[0:NZ, NZ:] = -wz[NZ:, 0:NZ]
        maps_wait(0)

    plan.add("tables", tables_wait, after=[("m2", j) for j in range(4)],
             needs=[("m2", j) for j in range(4)], rank=0)

    plan.add("maps1", lambda: maps_wait(1), needs=["m2b"], after=["tables"], rank=0)
    plan.add("w1", weights1, after=[("own", 1)], cost=2.0, rank=6)
    plan.add("w2", lambda: pl.loop(0, 3)(weights2), after=["w1"], cost=1.6, rank=7)

    def block(e, x):
        mask = samp[e].astype(F32)
        wide = lambda v: v.astype(F32).reshape(NZ, NY)
        mr, mi = wide(M[:, 0, x]), wide(M[:, 1, x])
        ir, ii = wide(G[e, :, 0, x]), wide(G[e, :, 1, x])
        pr = (mr * ir - mi * ii).astype(BF)
        pi = (mr * ii + mi * ir).astype(BF)
        r = mm(wy[...], jnp.concatenate([pr, pi], axis=1), NT).astype(BF)
        rc = jnp.concatenate([r[:NY], r[NY:]], axis=1)
        sp = mm(rc, wz[...], NN)
        dr = (mask * (sp[:, :NZ] - meas[e, 0, x].astype(F32))).astype(BF)
        di = (mask * (sp[:, NZ:] - meas[e, 1, x].astype(F32))).astype(BF)
        res[:, :NZ] = dr
        res[:, NZ:] = di

    def block_back(e, x):
        wide = lambda v: v.astype(F32).reshape(NZ, NY)
        mr, mi = wide(M[:, 0, x]), wide(M[:, 1, x])
        b = mm(wz[...], res[...], NT).astype(BF)
        bc = jnp.concatenate([b[:NZ], b[NZ:]], axis=1)
        im = mm(bc, wy[...], NN)
        br, bi = im[:, :NY], im[:, NY:]
        cells = (2, 8, 2, 8, NY)
        gd[e, :, :, :, 0, x] = (mr * br + mi * bi).reshape(cells).astype(BF)
        gd[e, :, :, :, 1, x] = (mr * bi - mi * br).reshape(cells).astype(BF)

    def sib_copy(e):
        return rcopy(gd.at[e, :, :, 1 - c], sibbuf.at[e], bcs.at[e], bcr.at[e], sib, p)

    def last_block(e):
        block_back(e, 1)
        sib_copy(e).start()

    def back_copy(h, e, col, d):
        src, dst = sbuf.at[h, col, d, e], rbuf.at[h, col, d, e]
        if h == 0:
            src, dst = src.at[d], dst.at[d]
        return rcopy(src, dst, brs.at[e], brr.at[h, col, d, e], ring[d], p)

    def x_copy(e):
        return rcopy(xsb.at[e], xrb.at[e], bxs.at[e], bxr.at[e], xp, p)

    def pair_sum(e):
        sib_copy(e).wait_recv()
        S[e] = gd[e, :, :, c].astype(F32) + sibbuf[e].astype(F32)
        if e in X_FIRST:
            xsb8[e] = S[e, 1 - xh].astype(BF)
            x_copy8(e).start()
        else:
            first_hop(e, (1, 0))

    def first_hop(e, cols):
        for col in cols:
            for d in range(2):
                sbuf[0, col, d, e, d] = S[e, (xh + col) % 2, (z + 4) % 8, d].astype(BF)
                back_copy(0, e, col, d).start()

    def x_copy8(e):
        return rcopy(xsb8.at[e], xrb8.at[e], bxs.at[e], bxr.at[e], xp, p)

    def x_sum(e):
        x_copy8(e).wait_recv()
        S[e, xh] = S[e, xh] + xrb8[e].astype(F32)
        first_hop(e, (0,))

    def back_hop(e, h, col):
        for d in range(2):
            back_copy(h - 1, e, col, d).wait_recv()
            k = 4 - h
            tz = (z + k) % 8 if d == 0 else (z + 8 - k) % 8
            lane = (xh + col) % 2
            if h == 1:
                v = S[e, lane, tz, d] + rbuf[0, col, d, e, d].astype(F32)
                sbuf[1, col, d, e, d] = v.astype(BF)
                sbuf[1, col, d, e, 1 - d] = S[e, lane, tz, 1 - d].astype(BF)
            else:
                v = S[e, lane, tz] + rbuf[h - 1, col, d, e].astype(F32)
                sbuf[h, col, d, e] = v.astype(BF)
            back_copy(h, e, col, d).start()

    def back_end(e, col):
        for d in range(2):
            back_copy(3, e, col, d).wait_recv()
        lane = (xh + col) % 2
        v = S[e, lane, z] + rbuf[3, col, 0, e].astype(F32) + rbuf[3, col, 1, e].astype(F32)
        if col == 1:
            xsb[e] = v.astype(BF)
            x_copy(e).start()
        else:
            S[e, lane, z] = v

    def u_copy(i, e):
        q = OFFSETS[i]
        return rcopy(U.at[2, e], U.at[2 - q, e], us.at[i, e], ur.at[i, e], s, p + q)

    def e_copy(i, q, e):
        k = 5 * i + q + 2
        return rcopy(esend.at[i, e], erecv.at[i, 2 - q, e], es.at[k, e], er.at[k, e], (s + 1, s - 1)[i], p + q)

    def all_halo(act, inward):
        for i, cond in enumerate((has_up, has_down) if inward else (has_down, has_up)):
            for q in (-2, 2, -1, 1, 0):
                both = jnp.logical_and(cond, phase_there(-q if inward else q))
                pl.when(both)(lambda: act(lambda e: e_copy(i, q, e)))
        for i, q in enumerate(OFFSETS):
            pl.when(phase_there(-q if inward else q))(lambda: act(lambda e: u_copy(i, e)))

    def update(e):
        g = S[e, xh, z]
        if e not in X_FIRST:
            x_copy(e).wait_recv()
            g = g + xrb[e].astype(F32)
        u = (img[e].astype(F32) - g).astype(BF)
        U[2, e] = u
        v = u.astype(F32)
        for i, first in enumerate((6, 0)):
            for r in range(2):
                for x in range(2):
                    k = 4 * r + 2 * x
                    esc[i, e, k : k + 2] = v[r, x, first : first + 2]
            esend[i, e] = esc[i, e].astype(BF)
        all_halo(lambda copy: copy(e).start(), False)

    lane = lax.broadcasted_iota(jnp.int32, (32, NY), 1)

    def columns(e):
        all_halo(lambda copy: copy(e).wait_recv(), True)
        V, rows, part0 = (VB, 32, 0) if isinstance(e, int) else (VA, 128, e * 32)

        @pl.loop(0, 5)
        def _(q):
            there = jnp.logical_and(p + q >= 2, p + q < PHASES + 2)
            up = jnp.where(has_up, erecv[0, q, e].astype(F32), 0.0)
            down = jnp.where(has_down, erecv[1, q, e].astype(F32), 0.0)
            for x in range(2):
                col_s[:, 2:10] = U[q, e, :, x].astype(F32)
                for r in range(2):
                    k = 4 * r + 2 * x
                    col_s[r, 0:2] = up[k : k + 2]
                    col_s[r, 10:12] = down[k : k + 2]
                v = jnp.where(there, col_s[...].reshape(32, NY), 0.0)
                back = jnp.where(lane == 0, 0.0, pltpu.roll(v, 1, 1))
                ahead = jnp.where(lane == NY - 1, 0.0, pltpu.roll(v, NY - 1, 1))
                for d, part in enumerate((back, v, ahead)):
                    first = pl.multiple_of((q * 3 + d) * rows + part0, 32)
                    V[pl.ds(first, 32), x * NY : (x + 1) * NY] = part.astype(BF)

    def conv_part(t):
        cells = VA[pl.ds(pl.multiple_of(t * 384, 384), KA), :]
        hacc[t] = mm(W1A[...], cells, NN) + b1_s[...]

    before = []
    later = ["maps1"]
    for e in range(E):
        for x in range(2):
            plan.add(("dft", e, x), lambda e=e, x=x: block(e, x), after=["tables", ("full", e)] + before + later * x,
                     cost=0.93, rank=20 + e)
            before = [("back", e, x)]
            plan.add(before[0], lambda e=e, x=x: last_block(e) if x else block_back(e, 0),
                     after=[("dft", e, x)], cost=0.93, sends=[(("bc", e), "c", 16)] * x, rank=20 + e)
        cols = (0,) if e in X_FIRST else (1, 0)
        starts = [(("b", e, col, 0), "z%d" % d, 0.5) for col in cols for d in range(2)]
        if e in X_FIRST:
            plan.add(("pair", e), lambda e=e: pair_sum(e), after=[("back", e, 1)], needs=[("bc", e)], cost=0.25,
                     sends=[(("bx", e), "x", 8)], rank=10 + e)
            plan.add(("xsum", e), lambda e=e: x_sum(e), after=[("pair", e)], needs=[("bx", e)], cost=0.15,
                     sends=starts, rank=10 + e)
        else:
            plan.add(("pair", e), lambda e=e: pair_sum(e), after=[("back", e, 1)], needs=[("bc", e)], cost=0.25,
                     sends=starts, rank=10 + e)
        for h in range(1, 4):
            for col in cols:
                plan.add(("back", e, h, col), lambda e=e, h=h, col=col: back_hop(e, h, col),
                         needs=[("b", e, col, h - 1)], after=[("pair", e)] + [("back", e, h, 1)] * ((1 - col) * (len(cols) - 1)),
                         sends=[(("b", e, col, h), "z%d" % d, 1) for d in range(2)], cost=0.03, rank=10 + e)
        for col in cols:
            plan.add(("end", e, col), lambda e=e, col=col: back_end(e, col), needs=[("b", e, col, 3)],
                     after=[("back", e, 3, col)], sends=[(("bx", e), "x", 1)] * col, cost=0.1, rank=10 + e)
        plan.add(("upd", e), lambda e=e: update(e), needs=[("bx", e)], after=[("end", e, 0)], cost=0.05,
                 sends=[(("e", e), "e", 1), (("u", e), "y", 1)], rank=10 + e)
    plan.add("cols", lambda: pl.loop(0, 4)(columns), needs=[(k, 3) for k in "ue"], after=[("upd", 4)], cost=1.0)
    plan.add("conv", lambda: pl.loop(0, 3)(conv_part), after=["cols"], cost=5.6, rank=30)
    plan.add("cols4", lambda: columns(4), needs=[(k, 4) for k in "ue"], after=["cols"], cost=0.25, rank=40)

    plan.run()

    rows = lax.broadcasted_iota(jnp.int32, (640, 2 * NY), 0)
    lowest = jnp.where(s == 0, FEAT, 0)
    highest = jnp.where(s == SLABS - 1, 9 * FEAT, 10 * FEAT)

    @pl.loop(0, 3)
    def _(t):
        there = jnp.logical_and(p + t >= 1, p + t < PHASES + 1)
        cells = VB[pl.ds(pl.multiple_of(t * 96, 96), KB), :]
        h = mm(W1B[...], cells, NN) + hacc[t]
        keep = jnp.logical_and(jnp.logical_and(rows >= lowest, rows < highest), there)
        first = pl.multiple_of(t * 640, 640)
        hid[pl.ds(first, 640), :] = jnp.where(keep, jnp.maximum(h, 0.0), 0.0).astype(BF)

    o = mm(W2[...], hid[...], NN)
    lane2 = lax.broadcasted_iota(jnp.int32, (128, 2 * NY), 1) % NY
    total = (
        o[128:256]
        + jnp.where(lane2 == 0, 0.0, pltpu.roll(o[:128], 1, 1))
        + jnp.where(lane2 == NY - 1, 0.0, pltpu.roll(o[256:], 2 * NY - 1, 1))
    )
    for k in range(6):
        osc[k] = total[:, k * 128 : (k + 1) * 128]
    for i in range(10):
        for x in range(2):
            second = jnp.concatenate(
                [osc[3 * x + k, pl.ds(i, 8, stride=16), :] for k in range(3)], axis=1
            )
            v = U[2, i // 2, i % 2, x].astype(F32) + second + b2_ref[i]
            out_ref[i // 2, i % 2, x] = v.astype(BF)

    for j in range(4):
        delta = p + 8 * j
        far = (s + delta) % 32

        @pl.when(delta != 0)
        def _():
            rcopy(maps.at[far], M.at[s], s1s.at[j], s1r.at[j], far, p).wait_send()

    for x in range(2):
        rcopy(G.at[0, 0:14], G.at[0, 0:14], s2s.at[x], s2r.at[0, 0, 0], s, p).wait_send()

    def left(e, n, sem):
        rcopy(G.at[e, 0:n], G.at[e, 0:n], sem.at[e], cr.at[e], sib, p).wait_send()

    for e in range(E):
        left(e, 7 if e in Z_FIRST else 14, rs)
        left(e, 8 if e in Z_FIRST else 1, xs)
        left(e, 7 if e in X_FIRST else 14, brs)
        left(e, 8 if e in X_FIRST else 1, bxs)

    @pl.loop(0, E)
    def _(e):
        left(e, 16, cs)
        sib_copy(e).wait_send()
        all_halo(lambda copy: copy(e).wait_send(), False)


def whole_step(img, maps, meas, samp, wy, wz, w1, b1, w2, b2):
    sem = pltpu.SemaphoreType.DMA
    vm = pl.BlockSpec(memory_space=pltpu.VMEM)
    far = pl.BlockSpec(memory_space=pl.ANY)
    v = pltpu.VMEM
    return pl.pallas_call(
        kernel,
        out_shape=jax.ShapeDtypeStruct((E, 2, 2, 8, NY), BF),
        in_specs=[far] * 7 + [vm, far, pl.BlockSpec(memory_space=pltpu.SMEM)],
        out_specs=vm,
        scratch_shapes=[
            v((E, 2, 2, 8, NY), BF),
            v((E, SLABS, 2, 2, 8, NY), BF),
            v((SLABS, 2, 2, 8, NY), BF),
            v((E, 2, 2, NY, NZ), BF),
            v((E, NY, NZ), jnp.int32),
            v((2 * NY, 2 * NY), BF),
            v((2 * NZ, 2 * NZ), BF),
            v((E, 2, 8, 2, 2, 2, 8, NY), BF),
            v((E, 2, 8, 2, 2, 8, NY), BF),
            v((E, 2, 8, 2, 2, 8, NY), F32),
            v((4, 2, 2, E, 2, 2, 8, NY), BF),
            v((4, 2, 2, E, 2, 2, 8, NY), BF),
            v((E, 2, 2, 8, NY), BF),
            v((E, 2, 2, 8, NY), BF),
            v((3, 8, 2, 2, 8, NY), BF),
            v((3, 8, 2, 2, 8, NY), BF),
            v((NY, 2 * NZ), BF),
            v((2, E, 8, NY), F32),
            v((2, E, 8, NY), BF),
            v((2, 5, E, 8, NY), BF),
            v((5, E, 2, 2, 8, NY), BF),
            v((270, FEAT), BF),
            v((27 * FEAT, 10), BF),
            v((640, KA), BF),
            v((640, KB), BF),
            v((384, K2), BF),
            v((640, 1), F32),
            v((16, K2), F32),
            v((2, 16, NY), F32),
            v((15 * 128, 2 * NY), BF),
            v((15 * 32, 2 * NY), BF),
            v((3, 640, 2 * NY), F32),
            v((1920, 2 * NY), BF),
            v((6, 128, 128), F32),
            sem((E,)), sem((E,)),
            sem((E,)), sem((E, 2, 2, 4)),
            sem((E,)), sem((E,)),
            sem((4,)), sem((4,)),
            sem((2,)), sem((2, 4, 7)),
            sem((12,)),
            sem((E,)), sem((E,)),
            sem((E,)), sem((4, 2, 2, E)),
            sem((E,)), sem((E,)),
            sem((10, E)), sem((10, E)),
            sem((4, E)), sem((4, E)),
        ],
        compiler_params=pltpu.CompilerParams(
            collective_id=0, has_side_effects=True, vmem_limit_bytes=62 * 1024 * 1024
        ),
        name="whole_step",
    )(img, maps, meas, samp, wy, wz, w1, b1, w2, b2)


def on_device(
    current_image,
    coil_maps,
    measured,
    sampling,
    first_weight,
    first_bias,
    second_weight,
    second_bias,
):
    wy, wz = tables()
    out = whole_step(
        current_image[0], coil_maps, measured[0, 0], sampling[0],
        jnp.asarray(wy), jnp.asarray(wz), first_weight.transpose(1, 2, 3, 4, 0).reshape(270, FEAT),
        first_bias[None], second_weight.transpose(1, 2, 3, 4, 0).reshape(27 * FEAT, 10), second_bias,
    )
    return out[None]


def solution(mesh):
    in_specs = (
        P("coil", None, None, None, "slab", None),
        P(None, None, None, "slab", None),
        P("coil", "slab", None, None, None, None, None),
        P("coil", None, None, None),
        P(),
        P(),
        P(),
        P(),
    )
    out_specs = P("coil", None, None, None, "slab", None)
    return jax.shard_map(
        on_device, mesh=mesh, in_specs=in_specs, out_specs=out_specs, check_vma=False
    )
```
